32 devices in a mesh: dp: 4 (over y, x), seq: 8 (over z, core).
Axes of the slice: x: 2, y: 2, z: 4, core: 2. Of those that a mesh axis runs over, the one named last changes fastest.
Arguments:
- inputs: bfloat16 [4, 1024, 1600], P('dp', 'seq'), may hold values from -6 to 6
- segment_ids: int32 [4, 1024], P('dp', 'seq'), may hold values from 0 to 3, never falling along the last dimension, each value on 1 to 512 neighbouring positions
- cotangent: bfloat16 [4, 1024, 1600], P('dp', 'seq'), may hold values from -6 to 6
- attn_gain: bfloat16 [1600], P('seq'), may hold values from 0.5 to 1.5
- attn_shift: bfloat16 [1600], P('seq'), may hold values from -2 to 2
- qkv_weight: bfloat16 [1600, 4800], P('dp', 'seq'), may hold values from -0.15625 to 0.15625
- query_bias: bfloat16 [1600], P('seq'), may hold values from -2 to 2
- value_bias: bfloat16 [1600], P('seq'), may hold values from -2 to 2
- out_weight: bfloat16 [1600, 1600], P('dp', 'seq'), may hold values from -0.625 to 0.625
- out_bias: bfloat16 [1600], P('seq'), may hold values from -2 to 2
- mlp_gain: bfloat16 [1600], P('seq'), may hold values from 0.5 to 1.5
- mlp_shift: bfloat16 [1600], P('seq'), may hold values from -2 to 2
- up_weight: bfloat16 [1600, 6400], P('dp', 'seq'), may hold values from -0.15625 to 0.15625
- up_bias: bfloat16 [6400], P('seq'), may hold values from -2 to 2
- down_weight: bfloat16 [6400, 1600], P('dp', 'seq'), may hold values from -0.078125 to 0.078125
- down_bias: bfloat16 [1600], P('seq'), may hold values from -2 to 2
Outputs:
- output: bfloat16 [4, 1024, 1600], P('dp', 'seq')
- grad_inputs: float32 [4, 1024, 1600], P('dp', 'seq')
- grad_attn_gain: float32 [1600], P('seq')
- grad_attn_shift: float32 [1600], P('seq')
- grad_qkv_weight: float32 [1600, 4800], P('dp', 'seq')
- grad_query_bias: float32 [1600], P('seq')
- grad_value_bias: float32 [1600], P('seq')
- grad_out_weight: float32 [1600, 1600], P('dp', 'seq')
- grad_out_bias: float32 [1600], P('seq')
- grad_mlp_gain: float32 [1600], P('seq')
- grad_mlp_shift: float32 [1600], P('seq')
- grad_up_weight: float32 [1600, 6400], P('dp', 'seq')
- grad_up_bias: float32 [6400], P('seq')
- grad_down_weight: float32 [6400, 1600], P('dp', 'seq')
- grad_down_bias: float32 [1600], P('seq')
The draws below stay inside these ranges and needn't reach their ends.
Inputs may be any that keep to these rules, and one draw needn't show every extreme that they name: `segment_ids`: along each sequence the ids never fall; each document holds 1 to 512 tokens, and some document holds exactly that many.
All inputs are finite; a program needn't handle non-finite values.
Results may differ from the reference program's by a relative error of at most 0.011.
Values may be sent and summed in bfloat16 or wider, within the bound.
A program may use at most 320 MiB of HBM per device.

```python
import math
import jax
import jax.numpy as jnp
import numpy as np
from jax import lax

D = 1600
HEADS = 25
HEAD_DIM = 64
FF = 6400
SEQ_LEN = 1024
BATCH = 4
DOCS = 4


def block_scale(rng, shape, cuts, least, high):
    def one(axis_at, parts):
        heights = jax.random.uniform(jax.random.fold_in(jax.random.fold_in(rng, 6), axis_at), (parts,), jnp.float32, least / len(cuts), high / len(cuts))
        return jnp.repeat(jnp.exp(heights), shape[axis_at] // parts).reshape((-1,) + (1,) * (len(shape) - axis_at - 1))

    level = one(*cuts[0])
    for cut in cuts[1:]:
        level = level * one(*cut)
    return level


def split_up(count, total, limit, lean):
    weights = [(1 << 20) // math.isqrt(rank ** lean) + 1 for rank in range(2, count + 1)]
    rest, holding = total - limit - (count - 1), [1] * (count - 1)
    while rest > 0:
        candidates = [i for i in range(count - 1) if holding[i] < limit]
        pool, budget = sum([weights[i] for i in candidates]), rest
        for i in candidates:
            extra = min(limit - holding[i], max(1, budget * weights[i] // pool), rest)
            holding[i] = holding[i] + extra
            rest = rest - extra
    return np.array([limit] + holding)


def ragged(key, amount, total, most, skew):
    if amount == 2:
        one = jax.random.randint(key, (), max(1, total - most), min(most, total - 1) + 1)
        return jnp.stack([one, total - one])
    lengths = jnp.asarray(split_up(amount, total, most, skew), jnp.int32)
    couples = (amount - 1) // 2
    giver, taker = lengths[1:1 + 2 * couples:2], lengths[2:2 + 2 * couples:2]
    slack = jnp.minimum(giver - 1, most - taker)
    shifted = jax.random.randint(jax.random.fold_in(key, 1), (couples,), 0, 1 << 20) % (slack + 1)
    lengths = lengths.at[1:1 + 2 * couples:2].set(giver - shifted).at[2:2 + 2 * couples:2].set(taker + shifted)
    return lengths[jax.random.permutation(jax.random.fold_in(key, 2), amount)]


def noise(rng, extent, scale, most, cuts=(), held_as=jnp.bfloat16):
    factor_of = block_scale(rng, extent, cuts, -0.22, 0.18) if cuts else 1.0
    array = jax.random.normal(rng, extent, jnp.float32) * scale * factor_of
    return jnp.minimum(jnp.maximum(array, -most), most).astype(held_as)


def setup_inputs(seed: int = 0) -> dict:
    streams_of = jax.random.split(jax.random.key(seed), 17)
    return {
        "inputs": noise(streams_of[0], (BATCH, SEQ_LEN, D), 1.0, 6.0, ((0, 4), (1, 8))),
        "segment_ids": jax.vmap(lambda own: jnp.searchsorted(jnp.cumsum(ragged(own, DOCS, SEQ_LEN, SEQ_LEN // 2, 2)), jnp.arange(SEQ_LEN), side="right"))(jax.random.split(streams_of[1], BATCH)).reshape((BATCH, SEQ_LEN)).astype(jnp.int32),
        "cotangent": noise(streams_of[2], (BATCH, SEQ_LEN, D), 1.0, 6.0, ((0, 4), (1, 8))),
        "attn_gain": jnp.clip(1.0 + 0.1 * jax.random.normal(streams_of[3], (D,), jnp.float32), 0.5, 1.5).astype(jnp.bfloat16),
        "attn_shift": noise(streams_of[4], (D,), 0.3, 2.0, ((0, 8),)),
        "qkv_weight": noise(streams_of[5], (D, 3 * D), D ** -0.5, 0.15625, ((0, 4), (1, 8))),
        "query_bias": noise(streams_of[6], (D,), 0.3, 2.0, ((0, 8),)),
        "value_bias": noise(streams_of[7], (D,), 0.3, 2.0, ((0, 8),)),
        "out_weight": noise(streams_of[8], (D, D), (D // 16) ** -0.5, 0.625, ((0, 4), (1, 8))),
        "out_bias": noise(streams_of[9], (D,), 0.3, 2.0, ((0, 8),)),
        "mlp_gain": jnp.clip(1.0 + 0.1 * jax.random.normal(streams_of[10], (D,), jnp.float32), 0.5, 1.5).astype(jnp.bfloat16),
        "mlp_shift": noise(streams_of[11], (D,), 0.3, 2.0, ((0, 8),)),
        "up_weight": noise(streams_of[12], (D, FF), D ** -0.5, 0.15625, ((0, 4), (1, 8))),
        "up_bias": noise(streams_of[13], (FF,), 0.3, 2.0, ((0, 8),)),
        "down_weight": noise(streams_of[14], (FF, D), FF ** -0.5, 0.078125, ((0, 4), (1, 8))),
        "down_bias": noise(streams_of[15], (D,), 0.3, 2.0, ((0, 8),)),
    }


@jax.custom_vjp
def low(v):
    return lax.optimization_barrier(v.astype(jnp.bfloat16)).astype(jnp.float32)

@jax.custom_vjp
def low_back(v):
    return v

def low_keep(v):
    return (low(v), None)

def low_pass(kept, grad):
    return (grad,)

def back_keep(v):
    return (v, None)

def back_low(kept, grad):
    return (low(grad),)
low.defvjp(low_keep, low_pass)
low_back.defvjp(back_keep, back_low)
highest = lax.Precision.HIGHEST

def layer_norm(values, gain, shift):
    center = values - lax.optimization_barrier(jnp.mean(values, axis=-1, keepdims=True))
    spread = lax.optimization_barrier(jnp.mean(center * center, axis=-1, keepdims=True))
    return center * lax.rsqrt(spread + 1e-05) * gain + shift

def project(values, weight):
    return jnp.einsum('bld,df->blf', values, weight, precision=highest)

def attend_sequence(queries, key_rows, value_rows, segment):
    length = queries.shape[0]
    span = min(512, length)
    blocks_total = length // span
    position = jnp.arange(length, dtype=jnp.int32)
    scaling = HEAD_DIM ** (-0.5)

    def one_block(portion):
        q_part, q_seg, q_pos = portion
        scores = jnp.einsum('qhd,khd->hqk', q_part, key_rows, precision=highest) * scaling
        scores = low_back(scores)
        visible = (q_seg[:, None] == segment[None, :]) & (position[None, :] <= q_pos[:, None])
        scores = jnp.where(visible[None], scores, -1e+30)
        weights = low(jax.nn.softmax(scores, axis=-1))
        return jnp.einsum('hqk,khd->qhd', weights, value_rows, precision=highest)
    pieces = (queries.reshape(blocks_total, span, HEADS, HEAD_DIM), segment.reshape(blocks_total, span), position.reshape(blocks_total, span))
    result = lax.map(jax.checkpoint(one_block), pieces)
    return result.reshape(length, HEADS * HEAD_DIM)

def layer(inputs, segment_ids, attn_gain, attn_shift, qkv_weight, query_bias, value_bias, out_weight, out_bias, mlp_gain, mlp_shift, up_weight, up_bias, down_weight, down_bias):
    normed = low(layer_norm(inputs, attn_gain, attn_shift))
    biases = jnp.concatenate([query_bias, jnp.zeros_like(query_bias), value_bias])
    mixed = low(low_back(project(normed, qkv_weight) + biases))
    batch_size, seq_length, width = inputs.shape
    split = mixed.reshape(batch_size, seq_length, 3, HEADS, HEAD_DIM)

    def per_sequence(portion):
        return attend_sequence(portion[0][:, 0], portion[0][:, 1], portion[0][:, 2], portion[1])
    attended = lax.map(per_sequence, (split, segment_ids))
    attended = low(low_back(attended))
    residual = inputs + low_back(project(attended, out_weight) + out_bias)
    second = low(layer_norm(residual, mlp_gain, mlp_shift))
    hidden = low_back(project(second, up_weight) + up_bias)
    activated = low(jax.nn.gelu(hidden, approximate=True))
    return residual + low_back(project(activated, down_weight) + down_bias)

def reference(inputs, segment_ids, cotangent, attn_gain, attn_shift, qkv_weight, query_bias, value_bias, out_weight, out_bias, mlp_gain, mlp_shift, up_weight, up_bias, down_weight, down_bias):
    floats = [item.astype(jnp.float32) for item in (inputs, attn_gain, attn_shift, qkv_weight, query_bias, value_bias, out_weight, out_bias, mlp_gain, mlp_shift, up_weight, up_bias, down_weight, down_bias)]

    def forward(f_inputs, f_attn_gain, f_attn_shift, f_qkv, f_query_bias, f_value_bias, f_out, f_out_bias, f_mlp_gain, f_mlp_shift, f_up, f_up_bias, f_down, f_down_bias):
        return layer(f_inputs, segment_ids, f_attn_gain, f_attn_shift, f_qkv, f_query_bias, f_value_bias, f_out, f_out_bias, f_mlp_gain, f_mlp_shift, f_up, f_up_bias, f_down, f_down_bias)
    output, pull = jax.vjp(forward, *floats)
    grads = pull(cotangent.astype(jnp.float32))
    return (output.astype(jnp.bfloat16), grads[0], grads[1], grads[2], grads[3], grads[4], grads[5], grads[6], grads[7], grads[8], grads[9], grads[10], grads[11], grads[12], grads[13])
```

```python
import functools

import jax
import jax.numpy as jnp
from jax import lax
from jax.experimental import pallas as pl
from jax.experimental.pallas import tpu as pltpu
from jax.sharding import PartitionSpec as P

HEADS = 25
HEAD_DIM = 64
CORES = 2
MESH = pl.DeviceIdType.MESH
F32 = jnp.float32
BF16 = jnp.bfloat16
ANY = pl.BlockSpec(memory_space=pl.ANY)
VMEM = pl.BlockSpec(memory_space=pltpu.VMEM)
VMEM_LIMIT = 60 * 1024 * 1024


def layer_norm(values, gain, shift):
    center = values - jnp.mean(values, axis=-1, keepdims=True)
    spread = jnp.mean(center * center, axis=-1, keepdims=True)
    return center * lax.rsqrt(spread + 1e-05) * gain + shift


def gelu_tanh(values):
    return jax.nn.gelu(values, approximate=True)


def dot(left, right, dims):
    return lax.dot_general(left, right, (dims, ((), ())), preferred_element_type=F32)


NN = ((1,), (0,))
NT = ((1,), (1,))
TN = ((0,), (0,))


class Plan:
    def __init__(self, nd, nq, tokens, width, ff):
        self.nd, self.nq, self.nc = nd, nq, nq // CORES
        self.tl, self.length, self.width, self.ff = tokens, tokens * nq, width, ff
        self.ratio = nq // nd
        self.slots = -(-HEADS // nq)
        self.kd = width // nd
        self.cq = width // nq
        self.fq = ff // nq
        self.gq = HEAD_DIM // nq
        self.go = HEAD_DIM // nd
        self.groups_q = 3 * self.slots * nq
        self.groups_o = self.slots * nd
        self.hw = self.slots * HEAD_DIM

    def owner(self, head):
        return (head * self.nq) // HEADS

    def first(self, q):
        return (HEADS * q + self.nq - 1) // self.nq

    def count(self, q):
        return self.first(q + 1) - self.first(q)


def here():
    return lax.axis_index("dp"), lax.axis_index("seq")


def remote(src, dst, send, recv, d, q):
    return pltpu.make_async_remote_copy(
        src_ref=src, dst_ref=dst, send_sem=send, recv_sem=recv, device_id=(d, q), device_id_type=MESH
    )


def local(src, dst, sem):
    return pltpu.make_async_copy(src, dst, sem)


def wait_for(ref, sem):
    pltpu.make_async_copy(ref, ref, sem).wait()


def signal(sem, d, q):
    pl.semaphore_signal(sem, inc=1, device_id=(d, q), device_id_type=MESH)


def greet_all(plan):
    d, q = here()
    me = d * plan.nq + q
    barrier = pltpu.get_barrier_semaphore()
    total = plan.nd * plan.nq

    def one(k, carry):
        other = lax.rem(me + k, total)
        signal(barrier, other // plan.nq, lax.rem(other, plan.nq))
        return carry

    lax.fori_loop(1, total, one, 0)
    pl.semaphore_wait(barrier, total - 1)


def greet_chain(plan):
    d, q = here()
    chip, core = q // CORES, lax.rem(q, CORES)
    barrier = pltpu.get_barrier_semaphore()
    signal(barrier, d, q + 1 - 2 * core)

    @pl.when(chip < plan.nc - 1)
    def _():
        signal(barrier, d, q + CORES)

    @pl.when(chip > 0)
    def _():
        signal(barrier, d, q - CORES)

    pl.semaphore_wait(barrier, 1 + jnp.minimum(chip, 1) + jnp.minimum(plan.nc - 1 - chip, 1))


class Gather:
    def __init__(self, plan, own, buf, send, recv, loc):
        self.plan, self.own, self.buf, self.send, self.recv, self.loc = plan, own, buf, send, recv, loc
        self.d, self.q = here()
        self.chip, self.core = self.q // CORES, lax.rem(self.q, CORES)

    @staticmethod
    def sems(plan):
        return [
            pltpu.SemaphoreType.DMA((3, plan.nc)),
            pltpu.SemaphoreType.DMA((plan.nq,)),
            pltpu.SemaphoreType.DMA,
        ]

    def push(self, src, origin, way):
        slot = origin * CORES + self.core
        to = (self.q + CORES, self.q - CORES, self.q + 1 - 2 * self.core)[way]
        return remote(
            src, self.buf.at[slot], self.send.at[way, origin], self.recv.at[slot], self.d, to
        )

    def start(self):
        @pl.when(self.chip < self.plan.nc - 1)
        def _():
            self.push(self.own, self.chip, 0).start()

        @pl.when(self.chip > 0)
        def _():
            self.push(self.own, self.chip, 1).start()

        self.push(self.own, self.chip, 2).start()
        local(self.own, self.buf.at[self.q], self.loc).start()

    def step(self, s):
        nc = self.plan.nc

        def arrive(origin, way):
            slot = origin * CORES + self.core
            wait_for(self.buf.at[slot], self.recv.at[slot])

            @pl.when((self.chip < nc - 1) if way == 0 else (self.chip > 0))
            def _():
                self.push(self.buf.at[slot], origin, way).start()

            self.push(self.buf.at[slot], origin, 2).start()

        @pl.when(self.chip >= s)
        def _():
            arrive(self.chip - s, 0)

        @pl.when(self.chip + s < nc)
        def _():
            arrive(self.chip + s, 1)

    def finish(self):
        nc = self.plan.nc
        wait_for(self.own, self.loc)
        for o in range(nc):
            slot = o * CORES + 1 - self.core
            wait_for(self.buf.at[slot], self.recv.at[slot])
        for o in range(nc):
            wait_for(self.own, self.send.at[2, o])

            @pl.when((o <= self.chip) & (self.chip < nc - 1))
            def _():
                wait_for(self.own, self.send.at[0, o])

            @pl.when((o >= self.chip) & (self.chip > 0))
            def _():
                wait_for(self.own, self.send.at[1, o])


class Scatter:
    def __init__(self, plan, part, swap, flow, run, sems):
        self.plan, self.part, self.swap, self.flow, self.run = plan, part, swap, flow, run
        self.s_swap, self.r_swap, self.s_flow, self.r_flow = sems
        self.d, self.q = here()
        self.chip, self.core = self.q // CORES, lax.rem(self.q, CORES)

    @staticmethod
    def scratch(plan):
        block = (plan.tl, plan.width)
        return [
            pltpu.VMEM((plan.nc, *block), BF16),
            pltpu.VMEM((2, plan.nc, *block), BF16),
            pltpu.VMEM((2, plan.nc, *block), BF16),
            pltpu.SemaphoreType.DMA((plan.nc,)),
            pltpu.SemaphoreType.DMA((plan.nc,)),
            pltpu.SemaphoreType.DMA((2, plan.nc)),
            pltpu.SemaphoreType.DMA((2, plan.nc)),
        ]

    def order(self):
        nc = self.plan.nc
        seen = []
        for k in range(nc):
            for o in (nc - 1 - k, k):
                if o not in seen:
                    seen.append(o)
        return seen

    def swap_out(self, o):
        remote(
            self.part.at[o * CORES + 1 - self.core],
            self.swap.at[o],
            self.s_swap.at[o],
            self.r_swap.at[o],
            self.d,
            self.q + 1 - 2 * self.core,
        ).start()

    def pair_sum(self, o):
        return self.part[o * CORES + self.core].astype(F32) + self.swap[o].astype(F32)

    def forward(self, o, way):
        plan, chip = self.plan, self.chip
        active = (chip < o) if way == 0 else (chip > o)
        inner = (chip > 0) if way == 0 else (chip < plan.nc - 1)
        to = self.q + CORES if way == 0 else self.q - CORES

        @pl.when(active)
        def _():
            self.run[way, o] = self.pair_sum(o).astype(BF16)

            @pl.when(inner)
            def _():
                wait_for(self.flow.at[way, o], self.r_flow.at[way, o])
                self.run[way, o] = (self.pair_sum(o) + self.flow[way, o].astype(F32)).astype(BF16)

            remote(
                self.run.at[way, o],
                self.flow.at[way, o],
                self.s_flow.at[way, o],
                self.r_flow.at[way, o],
                self.d,
                to,
            ).start()

    def start(self):
        for o in self.order():
            self.swap_out(o)

    def flows(self):
        nc = self.plan.nc
        for k in range(nc - 1):
            for o in sorted({nc - 1 - k, k}):
                pass
        waited = set()
        for k in range(nc):
            for o, way in ((nc - 1 - k, 0), (k, 1)):
                if o not in waited:
                    wait_for(self.swap.at[o], self.r_swap.at[o])
                    waited.add(o)
                self.forward(o, way)

    def finish(self, out):
        plan, nc, chip = self.plan, self.plan.nc, self.chip
        out[...] = self.pair_sum(chip)

        @pl.when(chip > 0)
        def _():
            wait_for(self.flow.at[0, chip], self.r_flow.at[0, chip])
            out[...] += self.flow[0, chip].astype(F32)

        @pl.when(chip < nc - 1)
        def _():
            wait_for(self.flow.at[1, chip], self.r_flow.at[1, chip])
            out[...] += self.flow[1, chip].astype(F32)

        for o in range(nc):
            wait_for(self.swap.at[o], self.s_swap.at[o])

            @pl.when(chip < o)
            def _():
                wait_for(self.run.at[0, o], self.s_flow.at[0, o])

            @pl.when(chip > o)
            def _():
                wait_for(self.run.at[1, o], self.s_flow.at[1, o])


class Spread:
    def __init__(self, plan, axis, buf, send, recv):
        self.axis, self.buf, self.send, self.recv = axis, buf, send, recv
        self.d, self.q = here()
        self.n = plan.nd if axis == "dp" else plan.nq
        self.me = self.d if axis == "dp" else self.q

    def other(self, k):
        return lax.rem(self.me + k, self.n)

    def place(self, i):
        return (i, self.q) if self.axis == "dp" else (self.d, i)

    def start(self, block_of):
        for k in range(1, self.n):
            to = self.other(k)
            remote(
                block_of(to), self.buf.at[self.me], self.send.at[k], self.recv.at[self.me], *self.place(to)
            ).start()

    def wait(self):
        for k in range(1, self.n):
            i = self.other(k)
            wait_for(self.buf.at[i], self.recv.at[i])

    def wait_sent(self):
        for k in range(1, self.n):
            wait_for(self.buf.at[self.me], self.send.at[k])


def dma(*shape):
    return pltpu.SemaphoreType.DMA(shape)


def move(src, dst, send, recv, d, q, mine):
    @pl.when(jnp.logical_not(mine))
    def _():
        remote(src, dst, send, recv, d, q).start()

    @pl.when(mine)
    def _():
        local(src, dst, recv).start()


def start_kernel(plan, *refs):
    (x_own, c_own, vec_own, seg_own, wq_own, wo_own, wu_own, wd_own) = refs[:8]
    (gx, gc, gv, gs, wq, wo, wu, wd) = refs[8:16]
    (zq, zo, *sem) = refs[16:]
    d, q = here()
    nd, nq, r = plan.nd, plan.nq, plan.ratio
    it = iter(sem)
    ag_x = Gather(plan, x_own, gx, next(it), next(it), next(it))
    ag_c = Gather(plan, c_own, gc, next(it), next(it), next(it))
    loc = next(it)
    sp_v = Spread(plan, "seq", gv, next(it), next(it))
    sp_s = Spread(plan, "seq", gs, next(it), next(it))
    q_send, q_recv = next(it), next(it)
    sp_q = Spread(plan, "dp", wq, next(it), next(it))
    o_send, o_recv = next(it), next(it)
    sp_o = Spread(plan, "dp", wo, next(it), next(it))
    d_send, d_recv = next(it), next(it)
    sp_d = Spread(plan, "dp", wd, next(it), next(it))
    sp_u = Spread(plan, "dp", wu, next(it), next(it))

    zq[...] = jnp.zeros_like(zq)
    zo[...] = jnp.zeros_like(zo)
    fills = [
        local(zq, wq.at[d, pl.ds((t * plan.slots + plan.slots - 1) * nq, nq)], loc.at[t])
        for t in range(3)
    ]
    fills += [
        local(zo, wo.at[d, s, pl.ds((plan.slots - 1) * nd, nd)], loc.at[3 + s]) for s in range(r)
    ]
    for fill in fills:
        fill.start()
    for fill in fills:
        fill.wait()
    greet_all(plan)

    ag_x.start()
    local(vec_own, gv.at[q], loc.at[0]).start()
    local(seg_own, gs.at[q], loc.at[1]).start()
    sp_v.start(lambda to: vec_own)
    sp_s.start(lambda to: seg_own)

    per_third = HEADS * nq
    per_dev = 3 * HEADS

    def qkv_group(j, carry):
        g = q * per_dev + j
        third = g // per_third
        rest = g - third * per_third
        head = rest // nq
        piece = rest - head * nq
        to = plan.owner(head)
        row = (third * plan.slots + head - plan.first(to)) * nq + piece
        move(wq_own.at[j], wq.at[d, row], q_send.at[j], q_recv, d, to, to == q)
        return carry

    lax.fori_loop(0, per_dev, qkv_group, 0)

    sp_u.start(lambda to: wu_own)
    local(wu_own, wu.at[d], loc.at[2]).start()

    for s in range(r):
        to_d, to_q = q // r, d * r + s
        mine = (to_d == d) & (to_q == q)
        move(
            wd_own.at[s],
            wd.at[to_d, lax.rem(q, r)],
            d_send.at[s],
            d_recv.at[lax.rem(q, r)],
            to_d,
            to_q,
            mine,
        )

    def out_group(j, carry):
        g = d * HEADS + j
        head = g // nd
        piece = g - head * nd
        to = plan.owner(head)
        row = (head - plan.first(to)) * nd + piece
        to_d = q // r
        mine = (to_d == d) & (to == q)
        move(wo_own.at[j], wo.at[to_d, lax.rem(q, r), row], o_send.at[j], o_recv, to_d, to, mine)
        return carry

    lax.fori_loop(0, HEADS, out_group, 0)
    ag_c.start()

    many = plan.count(q) == plan.slots
    few = jnp.logical_not(many)
    for cond, n in ((many, plan.slots), (few, plan.slots - 1)):

        @pl.when(cond)
        def _():
            wait_for(wq.at[0, pl.ds(0, 3 * n * nq)], q_recv)

    sp_q.start(lambda to: wq.at[d])
    ag_x.step(1)
    for cond, n in ((many, plan.slots), (few, plan.slots - 1)):

        @pl.when(cond)
        def _():
            wait_for(wo.at[0, :, pl.ds(0, n * nd)], o_recv)

    sp_o.start(lambda to: wo.at[d])
    for s in range(r):
        wait_for(wd.at[d, s], d_recv.at[s])
    sp_d.start(lambda to: wd.at[d])
    for s in range(2, plan.nc):
        ag_x.step(s)
    for s in range(1, plan.nc):
        ag_c.step(s)

    ag_x.finish()
    ag_c.finish()
    for sp in (sp_v, sp_s, sp_q, sp_o, sp_d, sp_u):
        sp.wait()
        sp.wait_sent()
    wait_for(vec_own, loc.at[0])
    wait_for(seg_own, loc.at[1])
    wait_for(wu_own, loc.at[2])

    def sent_q(j, carry):
        g = q * per_dev + j
        third = g // per_third
        head = (g - third * per_third) // nq

        @pl.when(plan.owner(head) != q)
        def _():
            wait_for(wq_own.at[0], q_send.at[j])

        return carry

    lax.fori_loop(0, per_dev, sent_q, 0)

    def sent_o(j, carry):
        to = plan.owner((d * HEADS + j) // nd)

        @pl.when(jnp.logical_not((q // r == d) & (to == q)))
        def _():
            wait_for(wo_own.at[0], o_send.at[j])

        return carry

    lax.fori_loop(0, HEADS, sent_o, 0)
    for s in range(r):

        @pl.when(jnp.logical_not((q // r == d) & (d * r + s == q)))
        def _():
            wait_for(wd_own.at[s], d_send.at[s])


def start_call(plan, x, c, vec, seg, wq, wo, wu, wd):
    nd, nq, r = plan.nd, plan.nq, plan.ratio
    shape = jax.ShapeDtypeStruct
    outs = (
        shape((nq, *x.shape), x.dtype),
        shape((nq, *c.shape), c.dtype),
        shape((nq, *vec.shape), vec.dtype),
        shape((nq, *seg.shape), seg.dtype),
        shape((nd, plan.groups_q, plan.gq, plan.kd), BF16),
        shape((nd, r, plan.groups_o, plan.go, plan.cq), BF16),
        shape((nd, *wu.shape), BF16),
        shape((nd, *wd.shape), BF16),
    )
    return pl.pallas_call(
        functools.partial(start_kernel, plan),
        out_shape=outs,
        in_specs=[VMEM] * 8,
        out_specs=[ANY] * 8,
        scratch_shapes=[
            pltpu.VMEM((nq, plan.gq, plan.kd), BF16),
            pltpu.VMEM((nd, plan.go, plan.cq), BF16),
            *Gather.sems(plan),
            *Gather.sems(plan),
            dma(3 + r),
            dma(nq),
            dma(nq),
            dma(nq),
            dma(nq),
            dma(3 * HEADS),
            pltpu.SemaphoreType.DMA,
            dma(nd),
            dma(nd),
            dma(HEADS),
            pltpu.SemaphoreType.DMA,
            dma(nd),
            dma(nd),
            dma(r),
            dma(r),
            dma(nd),
            dma(nd),
            dma(nd),
            dma(nd),
        ],
        compiler_params=pltpu.CompilerParams(
            collective_id=0, has_side_effects=True, vmem_limit_bytes=VMEM_LIMIT
        ),
        name="start",
    )(x, c, vec, seg, wq, wo, wu, wd)


def gather_kernel(plan, own, buf, *sem):
    greet_chain(plan)
    ag = Gather(plan, own, buf, *sem)
    ag.start()
    for s in range(1, plan.nc):
        ag.step(s)
    ag.finish()


def gather_call(plan, own, ident):
    return pl.pallas_call(
        functools.partial(gather_kernel, plan),
        out_shape=jax.ShapeDtypeStruct((plan.nq, *own.shape), own.dtype),
        in_specs=[VMEM],
        out_specs=ANY,
        scratch_shapes=Gather.sems(plan),
        compiler_params=pltpu.CompilerParams(
            collective_id=ident, has_side_effects=True, vmem_limit_bytes=VMEM_LIMIT
        ),
        name="gather",
    )(own)


def scatter_kernel(plan, n, *refs):
    parts, outs, scratch = refs[:n], refs[n : 2 * n], refs[2 * n :]
    greet_chain(plan)
    each = len(scratch) // n
    rs = [
        Scatter(plan, parts[i], *scratch[i * each : i * each + 3], scratch[i * each + 3 : (i + 1) * each])
        for i in range(n)
    ]
    for one in rs:
        one.start()
    for one in rs:
        one.flows()
    for one, out in zip(rs, outs):
        one.finish(out)


def scatter_call(plan, parts, ident):
    n = len(parts)
    return pl.pallas_call(
        functools.partial(scatter_kernel, plan, n),
        out_shape=[jax.ShapeDtypeStruct((plan.tl, plan.width), F32)] * n,
        in_specs=[VMEM] * n,
        out_specs=[VMEM] * n,
        scratch_shapes=Scatter.scratch(plan) * n,
        compiler_params=pltpu.CompilerParams(
            collective_id=ident, has_side_effects=True, vmem_limit_bytes=VMEM_LIMIT
        ),
        name="scatter",
    )(*parts)


def end_kernel(plan, *refs):
    (p_n1, g_u, g_d, g_q, g_o) = refs[:5]
    (out_n1, r_u, o_d, o_q, o_o) = refs[5:10]
    (r_d, r_q, r_o, s_d, s_q, s_o) = refs[10:16]
    swap, flow, run, *rest = refs[16:]
    rs_sems, sem = rest[:4], rest[4:]
    d, q = here()
    nd, nq, r = plan.nd, plan.nq, plan.ratio
    it = iter(sem)
    sp = [Spread(plan, "dp", buf, next(it), next(it)) for buf in (r_u, r_d, r_q, r_o)]
    loc = next(it)
    d_send, d_recv, q_send, q_recv, o_send, o_recv = (next(it) for _ in range(6))
    rs = Scatter(plan, p_n1, swap, flow, run, rs_sems)

    greet_all(plan)
    rs.start()
    parts = (g_u, g_d, g_q, g_o)
    for i in (1, 2, 3, 0):
        sp[i].start(lambda to, i=i: parts[i].at[to])
        local(parts[i].at[d], sp[i].buf.at[d], loc.at[i]).start()
    rs.flows()

    sp[1].wait()
    wait_for(r_d.at[d], loc.at[1])
    for s in range(r):
        total = r_d[0, s].astype(F32)
        for i in range(1, nd):
            total += r_d[i, s].astype(F32)
        s_d[s] = total.astype(BF16)
        to_d, to_q = q // r, d * r + s
        mine = (to_d == d) & (to_q == q)
        move(
            s_d.at[s], o_d.at[lax.rem(q, r)], d_send.at[s], d_recv.at[lax.rem(q, r)], to_d, to_q, mine
        )

    per_third = HEADS * nq
    per_dev = 3 * HEADS
    sp[2].wait()
    wait_for(r_q.at[d], loc.at[2])
    first, count = plan.first(q), plan.count(q)

    def qkv_group(k, carry):
        total = r_q[0, k].astype(F32)
        for i in range(1, nd):
            total += r_q[i, k].astype(F32)
        s_q[k] = total.astype(BF16)
        return carry

    lax.fori_loop(0, plan.groups_q, qkv_group, 0)

    def qkv_place(k):
        third = k // (plan.slots * nq)
        rest = k - third * (plan.slots * nq)
        slot = rest // nq
        g = third * per_third + first * nq + rest
        to = g // per_dev
        return slot, to, g - to * per_dev

    def qkv_send(k, carry):
        slot, to, j = qkv_place(k)

        @pl.when(slot < count)
        def _():
            move(s_q.at[k], o_q.at[j], q_send.at[k], q_recv, d, to, to == q)

        return carry

    lax.fori_loop(0, plan.groups_q, qkv_send, 0)

    sp[3].wait()
    wait_for(r_o.at[d], loc.at[3])

    def out_place(k):
        slot = k // nd
        g = first * nd + k
        to_d = g // HEADS
        return slot, to_d, g - to_d * HEADS

    for s in range(r):

        def out_group(k, carry):
            total = r_o[0, s, k].astype(F32)
            for i in range(1, nd):
                total += r_o[i, s, k].astype(F32)
            s_o[s, k] = total.astype(BF16)
            return carry

        lax.fori_loop(0, plan.groups_o, out_group, 0)

    for s in range(r):

        def out_send(k, carry):
            slot, to_d, j = out_place(k)
            to_q = d * r + s
            mine = (to_d == d) & (to_q == q)

            @pl.when(slot < count)
            def _():
                move(s_o.at[s, k], o_o.at[j], o_send.at[s, k], o_recv, to_d, to_q, mine)

            return carry

        lax.fori_loop(0, plan.groups_o, out_send, 0)

    sp[0].wait()
    wait_for(r_u.at[d], loc.at[0])
    rs.finish(out_n1)
    for s in range(r):
        wait_for(o_d.at[s], d_recv.at[s])
    wait_for(o_q, q_recv)
    wait_for(o_o, o_recv)
    for one in sp:
        one.wait_sent()

    for s in range(r):

        @pl.when(jnp.logical_not((q // r == d) & (d * r + s == q)))
        def _():
            wait_for(s_d.at[s], d_send.at[s])

    def sent_q(k, carry):
        slot, to, j = qkv_place(k)

        @pl.when((slot < count) & (to != q))
        def _():
            wait_for(s_q.at[0], q_send.at[k])

        return carry

    lax.fori_loop(0, plan.groups_q, sent_q, 0)
    for s in range(r):

        def sent_o(k, carry):
            slot, to_d, j = out_place(k)
            mine = (to_d == d) & (d * r + s == q)

            @pl.when((slot < count) & jnp.logical_not(mine))
            def _():
                wait_for(s_o.at[0, 0], o_send.at[s, k])

            return carry

        lax.fori_loop(0, plan.groups_o, sent_o, 0)


def end_call(plan, p_n1, g_u, g_d, g_q, g_o, ident):
    nd, nq, r = plan.nd, plan.nq, plan.ratio
    shape = jax.ShapeDtypeStruct
    return pl.pallas_call(
        functools.partial(end_kernel, plan),
        out_shape=(
            shape((plan.tl, plan.width), F32),
            shape(g_u.shape, BF16),
            shape(g_d.shape[1:], BF16),
            shape((3 * HEADS, plan.gq, plan.kd), BF16),
            shape((HEADS, plan.go, plan.cq), BF16),
        ),
        in_specs=[VMEM, ANY, ANY, ANY, ANY],
        out_specs=[VMEM, ANY, ANY, ANY, ANY],
        scratch_shapes=[
            pltpu.VMEM(g_d.shape, BF16),
            pltpu.VMEM(g_q.shape, BF16),
            pltpu.VMEM(g_o.shape, BF16),
            pltpu.VMEM(g_d.shape[1:], BF16),
            pltpu.VMEM(g_q.shape[1:], BF16),
            pltpu.VMEM(g_o.shape[1:], BF16),
            *Scatter.scratch(plan),
            *[dma(nd)] * 8,
            dma(4),
            dma(r),
            dma(r),
            dma(plan.groups_q),
            pltpu.SemaphoreType.DMA,
            dma(r, plan.groups_o),
            pltpu.SemaphoreType.DMA,
        ],
        compiler_params=pltpu.CompilerParams(
            collective_id=ident, has_side_effects=True, vmem_limit_bytes=VMEM_LIMIT
        ),
        name="end",
    )(p_n1, g_u, g_d, g_q, g_o)


def vector_kernel(plan, v_own, u_own, v_out, u_out, r_seq, r_dp, r_u, mid, *sem):
    d, q = here()
    greet_all(plan)
    it = iter(sem)
    sp_s = Spread(plan, "seq", r_seq, next(it), next(it))
    sp_d = Spread(plan, "dp", r_dp, next(it), next(it))
    sp_u = Spread(plan, "dp", r_u, next(it), next(it))
    sp_u.start(lambda to: u_own)
    sp_s.start(lambda to: v_own.at[to])
    sp_s.wait()
    total = v_own[q]
    for k in range(1, plan.nq):
        total += r_seq[sp_s.other(k)]
    mid[...] = total
    sp_d.start(lambda to: mid)
    sp_u.wait()
    sum_u = u_own[...]
    for k in range(1, plan.nd):
        sum_u += r_u[sp_u.other(k)]
    u_out[...] = sum_u
    sp_d.wait()
    for k in range(1, plan.nd):
        total += r_dp[sp_d.other(k)]
    v_out[...] = total
    for one in (sp_s, sp_d, sp_u):
        one.wait_sent()


def vector_call(plan, v, u, ident):
    nd, nq = plan.nd, plan.nq
    shape = jax.ShapeDtypeStruct
    return pl.pallas_call(
        functools.partial(vector_kernel, plan),
        out_shape=(shape(v.shape[1:], F32), shape(u.shape, F32)),
        in_specs=[VMEM] * 2,
        out_specs=[VMEM] * 2,
        scratch_shapes=[
            pltpu.VMEM(v.shape, F32),
            pltpu.VMEM((nd, *v.shape[1:]), F32),
            pltpu.VMEM((nd, *u.shape), F32),
            pltpu.VMEM(v.shape[1:], F32),
            dma(nq),
            dma(nq),
            dma(nd),
            dma(nd),
            dma(nd),
            dma(nd),
        ],
        compiler_params=pltpu.CompilerParams(
            collective_id=ident, has_side_effects=True, vmem_limit_bytes=VMEM_LIMIT
        ),
        name="vectors",
    )(v, u)


ROWS = 256


def visible(segc, segr, at, start, rows, keys):
    seen = segc[at : at + rows] == segr[:, start : start + keys]
    qpos = at + lax.broadcasted_iota(jnp.int32, (rows, keys), 0)
    kpos = start + lax.broadcasted_iota(jnp.int32, (rows, keys), 1)
    return seen & (kpos <= qpos)


def only(half, values):
    lane = lax.broadcasted_iota(jnp.int32, values.shape, 1)
    keep = (lane < HEAD_DIM) if half == 0 else (lane >= HEAD_DIM)
    return jnp.where(keep, values, jnp.zeros_like(values))


def either(first, second):
    lane = lax.broadcasted_iota(jnp.int32, first.shape, 1)
    return jnp.where(lane < HEAD_DIM, first, second)


def attend_kernel(plan, q_ref, k_ref, v_ref, segc, segr, o_ref, lse_ref):
    length, most = plan.length, plan.length // 2
    for at in range(0, length, ROWS):
        start = max(0, at - most)
        keys = at + ROWS - start
        mask = visible(segc, segr, at, start, ROWS, keys)
        query = q_ref[at : at + ROWS]
        key, value = k_ref[start : start + keys], v_ref[start : start + keys]
        outs, logs = [], []
        for half in range(2):
            scores = dot(only(half, query), key, NT) * (HEAD_DIM**-0.5)
            scores = jnp.where(mask, scores, -1e30)
            top = jnp.max(scores, axis=-1, keepdims=True)
            weights = jnp.exp(scores - top)
            total = jnp.sum(weights, axis=-1, keepdims=True)
            probs = (weights * (1.0 / total)).astype(BF16)
            outs.append(dot(probs, value, NN))
            logs.append(jnp.broadcast_to(top + jnp.log(total), (ROWS, 2 * HEAD_DIM)))
        o_ref[at : at + ROWS] = either(*outs).astype(BF16)
        lse_ref[at : at + ROWS] = either(*logs)


def attend_call(plan, mixed, segc, segr):
    pairs = plan.slots // 2
    block = lambda third: pl.BlockSpec((plan.length, 128), lambda i: (0, third * pairs + i))
    whole = lambda a: pl.BlockSpec(a.shape, lambda i: (0, 0))
    return pl.pallas_call(
        functools.partial(attend_kernel, plan),
        grid=(pairs,),
        out_shape=(
            jax.ShapeDtypeStruct((plan.length, plan.hw), BF16),
            jax.ShapeDtypeStruct((plan.length, plan.hw), F32),
        ),
        in_specs=[block(0), block(1), block(2), whole(segc), whole(segr)],
        out_specs=[block(0), block(0)],
        compiler_params=pltpu.CompilerParams(vmem_limit_bytes=VMEM_LIMIT),
        name="attend",
    )(mixed, mixed, mixed, segc, segr)


def attend_back_kernel(plan, q_ref, k_ref, v_ref, g_ref, lse_ref, segc, segr, dq, dk, dv, ak, av):
    length, most = plan.length, plan.length // 2
    scaling = HEAD_DIM**-0.5
    ak[...] = jnp.zeros_like(ak)
    av[...] = jnp.zeros_like(av)
    for at in range(0, length, ROWS):
        start = max(0, at - most)
        keys = at + ROWS - start
        mask = visible(segc, segr, at, start, ROWS, keys)
        query, grad = q_ref[at : at + ROWS], g_ref[at : at + ROWS]
        key, value = k_ref[start : start + keys], v_ref[start : start + keys]
        outs = []
        for half in range(2):
            query_h, grad_h = only(half, query), only(half, grad)
            scores = dot(query_h, key, NT) * scaling
            scores = jnp.where(mask, scores, -1e30)
            log = lse_ref[at : at + ROWS, half * HEAD_DIM : half * HEAD_DIM + 1]
            probs = jnp.exp(scores - log)
            grad_probs = dot(grad_h, value, NT)
            delta = jnp.sum(probs * grad_probs, axis=-1, keepdims=True)
            grad_scores = (probs * (grad_probs - delta)).astype(BF16)
            outs.append(dot(grad_scores, key, NN))
            ak[start : start + keys] += dot(grad_scores, query_h, TN)
            av[start : start + keys] += dot(probs.astype(BF16), grad_h, TN)
        dq[at : at + ROWS] = (either(*outs) * scaling).astype(BF16)
    dk[...] = (ak[...] * scaling).astype(BF16)
    dv[...] = av[...].astype(BF16)


def attend_back_call(plan, mixed, grad, lse, segc, segr):
    pairs = plan.slots // 2
    block = lambda third: pl.BlockSpec((plan.length, 128), lambda i: (0, third * pairs + i))
    whole = lambda a: pl.BlockSpec(a.shape, lambda i: (0, 0))
    return pl.pallas_call(
        functools.partial(attend_back_kernel, plan),
        grid=(pairs,),
        out_shape=[jax.ShapeDtypeStruct((plan.length, plan.hw), BF16)] * 3,
        in_specs=[block(0), block(1), block(2), block(0), block(0), whole(segc), whole(segr)],
        out_specs=[block(0)] * 3,
        scratch_shapes=[pltpu.VMEM((plan.length, 128), F32)] * 2,
        compiler_params=pltpu.CompilerParams(vmem_limit_bytes=VMEM_LIMIT),
        name="attend_back",
    )(mixed, mixed, mixed, grad, lse, segc, segr)


def shards(
    nd,
    nq,
    inputs,
    segment_ids,
    cotangent,
    attn_gain,
    attn_shift,
    qkv_weight,
    query_bias,
    value_bias,
    out_weight,
    out_bias,
    mlp_gain,
    mlp_shift,
    up_weight,
    up_bias,
    down_weight,
    down_bias,
):
    width = inputs.shape[2]
    plan = Plan(nd, nq, inputs.shape[1], width, up_weight.shape[1] * nq)
    r, slots, length = plan.ratio, plan.slots, plan.length
    q = lax.axis_index("seq")
    first, count = plan.first(q), plan.count(q)

    vec = jnp.stack(
        [attn_gain, attn_shift, query_bias, value_bias, out_bias, mlp_gain, mlp_shift, down_bias]
    )
    got = start_call(
        plan,
        inputs[0],
        cotangent[0],
        vec,
        segment_ids,
        qkv_weight.T.reshape(3 * HEADS, plan.gq, plan.kd),
        out_weight.reshape(HEADS, plan.go, plan.cq),
        up_weight,
        down_weight.T.reshape(plan.cq, r, plan.fq).transpose(1, 0, 2),
    )
    gx, gc, gv, gs, wq, wo, wu, wd = got
    xs = gx.reshape(length, width).astype(F32)
    cot = gc.reshape(length, width)
    v = gv.transpose(1, 0, 2).reshape(8, width).astype(F32)
    gain_one, shift_one, bias_query, bias_value, bias_out, gain_two, shift_two, bias_down = v
    segr = gs.reshape(1, length)
    segc = gs.reshape(length, 1)
    wq = wq.reshape(nd, 3 * plan.hw, plan.kd).transpose(1, 0, 2).reshape(3 * plan.hw, width)
    wo = wo.reshape(nd, r, plan.hw, plan.cq).transpose(2, 0, 1, 3).reshape(plan.hw, width)
    wu = wu.reshape(width, plan.fq)
    wd = wd.reshape(width, plan.fq)

    normed = layer_norm(xs, gain_one, shift_one).astype(BF16)
    mine = lambda b: lax.dynamic_slice(jnp.pad(b, (0, plan.hw)), (first * HEAD_DIM,), (plan.hw,))
    biases = jnp.concatenate([mine(bias_query), jnp.zeros((plan.hw,), F32), mine(bias_value)])
    mixed = (dot(normed, wq, NT) + biases).astype(BF16)
    attended, lse = attend_call(plan, mixed, segc, segr)
    part = dot(attended, wo, NN).astype(BF16).reshape(nq, plan.tl, width)
    (branch,) = scatter_call(plan, [part], 1)
    stream = inputs[0].astype(F32)
    residual = stream + branch + bias_out
    second = layer_norm(residual, gain_two, shift_two).astype(BF16)
    second_all = gather_call(plan, second, 2).reshape(length, width)
    hidden = dot(second_all, wu, NN) + up_bias.astype(F32)
    activated = gelu_tanh(hidden).astype(BF16)
    part_out = dot(activated, wd, NT).astype(BF16).reshape(nq, plan.tl, width)
    grad_act = dot(cot, wd, NN)
    grad_hidden = jax.vjp(gelu_tanh, hidden)[1](grad_act)[0].astype(BF16)
    part_second = dot(grad_hidden, wu, NT).astype(BF16).reshape(nq, plan.tl, width)
    down_sum, grad_second = scatter_call(plan, [part_out, part_second], 3)
    output = residual + down_sum + bias_down

    grad_resid, grad_gain_two, grad_shift_two = jax.vjp(layer_norm, residual, gain_two, shift_two)[
        1
    ](grad_second)
    top = cotangent[0].astype(F32)
    grad_resid = grad_resid + top
    grad_branch = grad_resid.astype(BF16)
    branch_all = gather_call(plan, grad_branch, 4).reshape(length, width)
    grad_attended = dot(branch_all, wo, NT).astype(BF16)
    dq, dk, dv = attend_back_call(plan, mixed, grad_attended, lse, segc, segr)
    grad_mixed = jnp.concatenate([dq, dk, dv], axis=1)
    part_one = dot(grad_mixed, wq, NN).astype(BF16).reshape(nq, plan.tl, width)

    g_u = dot(second_all, grad_hidden, TN).astype(BF16).reshape(nd, plan.kd, plan.fq)
    g_d = dot(cot, activated, TN).astype(BF16).reshape(nd, r, plan.cq, plan.fq)
    g_q = dot(grad_mixed, normed, TN).astype(BF16).reshape(3 * plan.hw, nd, plan.kd)
    g_q = g_q.transpose(1, 0, 2).reshape(nd, plan.groups_q, plan.gq, plan.kd)
    g_o = dot(attended, branch_all, TN).astype(BF16).reshape(plan.hw, nd, r, plan.cq)
    g_o = g_o.transpose(1, 2, 0, 3).reshape(nd, r, plan.groups_o, plan.go, plan.cq)
    grad_normed, r_u, o_d, o_q, o_o = end_call(plan, part_one, g_u, g_d, g_q, g_o, 5)
    grad_stream, grad_gain_one, grad_shift_one = jax.vjp(layer_norm, stream, gain_one, shift_one)[
        1
    ](grad_normed)
    grad_input = grad_stream + grad_resid

    def spread_heads(grad):
        sums = jnp.sum(grad.astype(F32), axis=0)
        sums = jnp.where(jnp.arange(plan.hw) < count * HEAD_DIM, sums, 0.0)
        full = jnp.zeros((width + plan.hw,), F32)
        return lax.dynamic_update_slice(full, sums, (first * HEAD_DIM,))[:width]

    vectors = jnp.stack(
        [
            grad_gain_one,
            grad_shift_one,
            spread_heads(dq),
            spread_heads(dv),
            jnp.sum(grad_branch.astype(F32), axis=0),
            grad_gain_two,
            grad_shift_two,
            jnp.sum(top, axis=0),
        ]
    )
    vectors = vectors.reshape(8, nq, plan.cq).transpose(1, 0, 2)
    up_sum = jnp.sum(grad_hidden.astype(F32), axis=0)[None]
    vectors, up_sum = vector_call(plan, vectors, up_sum, 6)
    grad_up = jnp.sum(r_u.astype(F32), axis=0)
    grad_down = o_d.astype(F32).transpose(0, 2, 1).reshape(r * plan.fq, plan.cq)
    grad_qkv = o_q.astype(F32).reshape(3 * HEADS * plan.gq, plan.kd).T
    grad_out = o_o.astype(F32).reshape(plan.kd, plan.cq)
    return (
        output.astype(BF16)[None],
        grad_input[None],
        vectors[0],
        vectors[1],
        grad_qkv,
        vectors[2],
        vectors[3],
        grad_out,
        vectors[4],
        vectors[5],
        vectors[6],
        grad_up,
        up_sum[0],
        grad_down,
        vectors[7],
    )


def solution(mesh):
    tokens, vector, matrix = P("dp", "seq", None), P("seq"), P("dp", "seq")
    return jax.shard_map(
        functools.partial(shards, mesh.shape["dp"], mesh.shape["seq"]),
        mesh=mesh,
        in_specs=(
            tokens,
            matrix,
            tokens,
            vector,
            vector,
            matrix,
            vector,
            vector,
            matrix,
            vector,
            vector,
            vector,
            matrix,
            vector,
            matrix,
            vector,
        ),
        out_specs=(
            tokens,
            tokens,
            vector,
            vector,
            matrix,
            vector,
            vector,
            matrix,
            vector,
            vector,
            vector,
            matrix,
            vector,
            matrix,
            vector,
        ),
        check_vma=False,
    )
```

```python
import functools

import jax
import jax.numpy as jnp
from jax import lax
from jax.experimental import pallas as pl
from jax.experimental.pallas import tpu as pltpu
from jax.sharding import PartitionSpec as P

HEADS = 25
HEAD_DIM = 64
CORES = 2
MESH = pl.DeviceIdType.MESH
F32 = jnp.float32
BF16 = jnp.bfloat16
ANY = pl.BlockSpec(memory_space=pl.ANY)
VMEM = pl.BlockSpec(memory_space=pltpu.VMEM)
VMEM_LIMIT = 60 * 1024 * 1024


def layer_norm(values, gain, shift):
    center = values - jnp.mean(values, axis=-1, keepdims=True)
    spread = jnp.mean(center * center, axis=-1, keepdims=True)
    return center * lax.rsqrt(spread + 1e-05) * gain + shift


def gelu_tanh(values):
    return jax.nn.gelu(values, approximate=True)


def dot(left, right, dims):
    return lax.dot_general(left, right, (dims, ((), ())), preferred_element_type=F32)


NN = ((1,), (0,))
NT = ((1,), (1,))
TN = ((0,), (0,))


class Plan:
    def __init__(self, nd, nq, tokens, width, ff):
        self.nd, self.nq, self.nc = nd, nq, nq // CORES
        self.tl, self.length, self.width, self.ff = tokens, tokens * nq, width, ff
        self.ratio = nq // nd
        self.slots = -(-HEADS // nq)
        self.kd = width // nd
        self.cq = width // nq
        self.fq = ff // nq
        self.gq = HEAD_DIM // nq
        self.go = HEAD_DIM // nd
        self.groups_q = 3 * self.slots * nq
        self.groups_o = self.slots * nd
        self.hw = self.slots * HEAD_DIM

    def owner(self, head):
        return (head * self.nq) // HEADS

    def first(self, q):
        return (HEADS * q + self.nq - 1) // self.nq

    def count(self, q):
        return self.first(q + 1) - self.first(q)


def here():
    return lax.axis_index("dp"), lax.axis_index("seq")


def remote(src, dst, send, recv, d, q):
    return pltpu.make_async_remote_copy(
        src_ref=src, dst_ref=dst, send_sem=send, recv_sem=recv, device_id=(d, q), device_id_type=MESH
    )


def local(src, dst, sem):
    return pltpu.make_async_copy(src, dst, sem)


def wait_for(ref, sem):
    pltpu.make_async_copy(ref, ref, sem).wait()


def signal(sem, d, q):
    pl.semaphore_signal(sem, inc=1, device_id=(d, q), device_id_type=MESH)


def greet_all(plan):
    d, q = here()
    me = d * plan.nq + q
    barrier = pltpu.get_barrier_semaphore()
    total = plan.nd * plan.nq

    def one(k, carry):
        other = lax.rem(me + k, total)
        signal(barrier, other // plan.nq, lax.rem(other, plan.nq))
        return carry

    lax.fori_loop(1, total, one, 0)
    pl.semaphore_wait(barrier, total - 1)


def greet_chain(plan):
    d, q = here()
    chip, core = q // CORES, lax.rem(q, CORES)
    barrier = pltpu.get_barrier_semaphore()
    signal(barrier, d, q + 1 - 2 * core)

    @pl.when(chip < plan.nc - 1)
    def _():
        signal(barrier, d, q + CORES)

    @pl.when(chip > 0)
    def _():
        signal(barrier, d, q - CORES)

    pl.semaphore_wait(barrier, 1 + jnp.minimum(chip, 1) + jnp.minimum(plan.nc - 1 - chip, 1))


def greet_near(plan):
    d, q = here()
    chip, core = q // CORES, lax.rem(q, CORES)
    barrier = pltpu.get_barrier_semaphore()
    signal(barrier, d, q + 1 - 2 * core)

    @pl.when(chip < plan.nc - 1)
    def _():
        signal(barrier, d, q + CORES)

    @pl.when(chip > 0)
    def _():
        signal(barrier, d, q - CORES)

    for k in range(1, plan.nd):
        signal(barrier, lax.rem(d + k, plan.nd), q)
    near = jnp.minimum(chip, 1) + jnp.minimum(plan.nc - 1 - chip, 1)
    pl.semaphore_wait(barrier, near + plan.nd)


def dma(*shape):
    return pltpu.SemaphoreType.DMA(shape)


class Gather:
    def __init__(self, plan, own, buf, send, recv, loc):
        self.plan, self.own, self.buf, self.send, self.recv, self.loc = plan, own, buf, send, recv, loc
        self.d, self.q = here()
        self.chip, self.core = self.q // CORES, lax.rem(self.q, CORES)

    @staticmethod
    def sems(plan):
        return [
            pltpu.SemaphoreType.DMA((3, plan.nc)),
            pltpu.SemaphoreType.DMA((plan.nq,)),
            pltpu.SemaphoreType.DMA,
        ]

    def push(self, src, origin, way):
        slot = origin * CORES + self.core
        to = (self.q + CORES, self.q - CORES, self.q + 1 - 2 * self.core)[way]
        return remote(
            src, self.buf.at[slot], self.send.at[way, origin], self.recv.at[slot], self.d, to
        )

    def start(self):
        @pl.when(self.chip < self.plan.nc - 1)
        def _():
            self.push(self.own, self.chip, 0).start()

        @pl.when(self.chip > 0)
        def _():
            self.push(self.own, self.chip, 1).start()

        self.push(self.own, self.chip, 2).start()
        local(self.own, self.buf.at[self.q], self.loc).start()

    def arrive(self, origin):
        slot = origin * CORES + self.core
        wait_for(self.buf.at[slot], self.recv.at[slot])

        @pl.when((origin < self.chip) & (self.chip < self.plan.nc - 1))
        def _():
            self.push(self.buf.at[slot], origin, 0).start()

        @pl.when((origin > self.chip) & (self.chip > 0))
        def _():
            self.push(self.buf.at[slot], origin, 1).start()

        self.push(self.buf.at[slot], origin, 2).start()

    def step(self, s):
        @pl.when(self.chip >= s)
        def _():
            self.arrive(self.chip - s)

        @pl.when(self.chip + s < self.plan.nc)
        def _():
            self.arrive(self.chip + s)

    def wait_own(self):
        wait_for(self.own, self.loc)

    def wait_partner(self, origin):
        slot = origin * CORES + 1 - self.core
        wait_for(self.buf.at[slot], self.recv.at[slot])

    def finish(self):
        self.wait_own()
        for o in range(self.plan.nc):
            self.wait_partner(o)
        self.sent()

    def sent(self):
        nc = self.plan.nc
        for o in range(nc):
            wait_for(self.own, self.send.at[2, o])

            @pl.when((o <= self.chip) & (self.chip < nc - 1))
            def _():
                wait_for(self.own, self.send.at[0, o])

            @pl.when((o >= self.chip) & (self.chip > 0))
            def _():
                wait_for(self.own, self.send.at[1, o])


class Scatter:
    def __init__(self, plan, part, swap, flow, run, sems):
        self.plan, self.part, self.swap, self.flow, self.run = plan, part, swap, flow, run
        self.s_swap, self.r_swap, self.s_flow, self.r_flow = sems
        self.d, self.q = here()
        self.chip, self.core = self.q // CORES, lax.rem(self.q, CORES)

    @staticmethod
    def scratch(plan):
        block = (plan.tl, plan.width)
        return [
            pltpu.VMEM((plan.nc, *block), BF16),
            pltpu.VMEM((2, plan.nc, *block), BF16),
            pltpu.VMEM((2, plan.nc, *block), BF16),
            pltpu.SemaphoreType.DMA((plan.nc,)),
            pltpu.SemaphoreType.DMA((plan.nc,)),
            pltpu.SemaphoreType.DMA((2, plan.nc)),
            pltpu.SemaphoreType.DMA((2, plan.nc)),
        ]

    def order(self):
        nc = self.plan.nc
        seen = []
        for k in range(nc):
            for o in (nc - 1 - k, k):
                if o not in seen:
                    seen.append(o)
        return seen

    def swap_out(self, o):
        remote(
            self.part.at[o * CORES + 1 - self.core],
            self.swap.at[o],
            self.s_swap.at[o],
            self.r_swap.at[o],
            self.d,
            self.q + 1 - 2 * self.core,
        ).start()

    def pair_sum(self, o):
        return self.part[o * CORES + self.core].astype(F32) + self.swap[o].astype(F32)

    def forward(self, o, way):
        plan, chip = self.plan, self.chip
        active = (chip < o) if way == 0 else (chip > o)
        inner = (chip > 0) if way == 0 else (chip < plan.nc - 1)
        to = self.q + CORES if way == 0 else self.q - CORES

        @pl.when(active)
        def _():
            self.run[way, o] = self.pair_sum(o).astype(BF16)

            @pl.when(inner)
            def _():
                wait_for(self.flow.at[way, o], self.r_flow.at[way, o])
                self.run[way, o] = (self.pair_sum(o) + self.flow[way, o].astype(F32)).astype(BF16)

            remote(
                self.run.at[way, o],
                self.flow.at[way, o],
                self.s_flow.at[way, o],
                self.r_flow.at[way, o],
                self.d,
                to,
            ).start()

    def start(self):
        for o in self.order():
            self.swap_out(o)

    def flows(self):
        nc = self.plan.nc
        for k in range(nc - 1):
            for o in sorted({nc - 1 - k, k}):
                pass
        waited = set()
        for k in range(nc):
            for o, way in ((nc - 1 - k, 0), (k, 1)):
                if o not in waited:
                    wait_for(self.swap.at[o], self.r_swap.at[o])
                    waited.add(o)
                self.forward(o, way)

    def finish(self, out):
        plan, nc, chip = self.plan, self.plan.nc, self.chip
        out[...] = self.pair_sum(chip)

        @pl.when(chip > 0)
        def _():
            wait_for(self.flow.at[0, chip], self.r_flow.at[0, chip])
            out[...] += self.flow[0, chip].astype(F32)

        @pl.when(chip < nc - 1)
        def _():
            wait_for(self.flow.at[1, chip], self.r_flow.at[1, chip])
            out[...] += self.flow[1, chip].astype(F32)

        for o in range(nc):
            wait_for(self.swap.at[o], self.s_swap.at[o])

            @pl.when(chip < o)
            def _():
                wait_for(self.run.at[0, o], self.s_flow.at[0, o])

            @pl.when(chip > o)
            def _():
                wait_for(self.run.at[1, o], self.s_flow.at[1, o])


class Spread:
    def __init__(self, plan, axis, buf, send, recv):
        self.axis, self.buf, self.send, self.recv = axis, buf, send, recv
        self.d, self.q = here()
        self.n = plan.nd if axis == "dp" else plan.nq
        self.me = self.d if axis == "dp" else self.q

    def other(self, k):
        return lax.rem(self.me + k, self.n)

    def place(self, i):
        return (i, self.q) if self.axis == "dp" else (self.d, i)

    def start(self, block_of):
        for k in range(1, self.n):
            to = self.other(k)
            remote(
                block_of(to), self.buf.at[self.me], self.send.at[k], self.recv.at[self.me], *self.place(to)
            ).start()

    def wait(self):
        for k in range(1, self.n):
            i = self.other(k)
            wait_for(self.buf.at[i], self.recv.at[i])

    def wait_sent(self):
        for k in range(1, self.n):
            wait_for(self.buf.at[self.me], self.send.at[k])


def move(src, dst, send, recv, d, q, mine):
    @pl.when(jnp.logical_not(mine))
    def _():
        remote(src, dst, send, recv, d, q).start()

    @pl.when(mine)
    def _():
        local(src, dst, recv).start()


class Flow:
    def __init__(self, plan, part, run, swap, flow, s_swap, r_swap, s_flow, r_flow):
        self.plan, self.part, self.run, self.swap, self.flow = plan, part, run, swap, flow
        self.s_swap, self.r_swap, self.s_flow, self.r_flow = s_swap, r_swap, s_flow, r_flow
        self.d, self.q = here()
        self.chip, self.core = self.q // CORES, lax.rem(self.q, CORES)

    @staticmethod
    def scratch(plan):
        block, nc = (plan.tl, plan.width), plan.nc
        return [
            pltpu.VMEM((nc, *block), BF16),
            pltpu.VMEM((nc, *block), BF16),
            pltpu.VMEM((nc, *block), BF16),
            pltpu.VMEM((nc + 1, *block), BF16),
            dma(nc),
            dma(nc),
            dma(nc),
            dma(nc + 1),
        ]

    def put(self, o, values):
        low, high = values[: self.plan.tl], values[self.plan.tl :]
        mine = self.core == 0
        self.run[o] = jnp.where(mine, low, high).astype(BF16)
        self.part[o] = jnp.where(mine, high, low).astype(BF16)
        remote(
            self.part.at[o],
            self.swap.at[o],
            self.s_swap.at[o],
            self.r_swap.at[o],
            self.d,
            self.q + 1 - 2 * self.core,
        ).start()

    def forward(self, o):
        plan, chip = self.plan, self.chip
        up = o > chip
        inner = jnp.where(up, chip > 0, chip < plan.nc - 1)
        to_chip = jnp.where(up, chip + 1, chip - 1)
        slot = jnp.where(jnp.logical_not(up) & (o == to_chip), plan.nc, o)
        wait_for(self.swap.at[o], self.r_swap.at[o])

        @pl.when(inner)
        def _():
            wait_for(self.flow.at[o], self.r_flow.at[o])
            total = self.run[o].astype(F32) + self.swap[o].astype(F32) + self.flow[o].astype(F32)
            self.run[o] = total.astype(BF16)

        @pl.when(jnp.logical_not(inner))
        def _():
            self.run[o] = (self.run[o].astype(F32) + self.swap[o].astype(F32)).astype(BF16)

        remote(
            self.run.at[o],
            self.flow.at[slot],
            self.s_flow.at[o],
            self.r_flow.at[slot],
            self.d,
            to_chip * CORES + self.core,
        ).start()

    def passes(self, which, near_first, skip=None):
        plan, chip = self.plan, self.chip
        up = (chip * 2 < plan.nc) if which == 0 else (chip * 2 >= plan.nc)

        def one(i, carry):
            k = i if near_first else plan.nc - 1 - i
            o = jnp.where(up, k, plan.nc - 1 - k)
            go = jnp.where(up, o > chip, o < chip)
            if skip is not None:
                go = go & jnp.logical_not(skip(o))

            @pl.when(go)
            def _():
                self.forward(o)

            return carry

        lax.fori_loop(0, plan.nc, one, 0)

    def finish(self, out):
        plan, nc, chip = self.plan, self.plan.nc, self.chip
        wait_for(self.swap.at[chip], self.r_swap.at[chip])
        out[...] = self.run[chip].astype(F32) + self.swap[chip].astype(F32)

        @pl.when(chip > 0)
        def _():
            wait_for(self.flow.at[chip], self.r_flow.at[chip])
            out[...] += self.flow[chip].astype(F32)

        @pl.when(chip < nc - 1)
        def _():
            wait_for(self.flow.at[nc], self.r_flow.at[nc])
            out[...] += self.flow[nc].astype(F32)

    def sent(self):
        for o in range(self.plan.nc):
            wait_for(self.swap.at[o], self.s_swap.at[o])

            @pl.when(self.chip != o)
            def _():
                wait_for(self.run.at[o], self.s_flow.at[o])


def nearest(plan, t):
    chip = lax.axis_index("seq") // CORES
    below, above = chip, plan.nc - 1 - chip
    both = jnp.minimum(below, above)
    s = jnp.where(t <= 2 * both, (t + 1) // 2, t - both)
    down = jnp.where(t <= 2 * both, lax.rem(t, 2) == 1, below > above)
    return jnp.where(down, chip - s, chip + s)


def norm_back(values, gain, grad):
    center = values - jnp.mean(values, axis=-1, keepdims=True)
    spread = jnp.mean(center * center, axis=-1, keepdims=True)
    inverse = lax.rsqrt(spread + 1e-05)
    hat = center * inverse
    scaled = grad * gain
    inner = jnp.mean(scaled, axis=-1, keepdims=True)
    outer = jnp.mean(scaled * hat, axis=-1, keepdims=True)
    back = (scaled - inner - hat * outer) * inverse
    return back, jnp.sum(grad * hat, axis=0, keepdims=True), jnp.sum(grad, axis=0, keepdims=True)


ROOT = 0.7978845608028654
CUBE = 0.044715


def gelu_both(h):
    t = jnp.tanh(ROOT * (h + CUBE * (h * h * h)))
    half = 0.5 * (1.0 + t)
    slope = half + 0.5 * h * (1.0 - t * t) * (ROOT * (1.0 + 3.0 * CUBE * (h * h)))
    return h * half, slope


LANES = 512


def mlp_kernel(plan, *refs):
    (n_own, resid, c_own, cot, wu, wd, rows, ub) = refs[:8]
    (out, gres, branch, r_u, r_d, vec, up_sum) = refs[8:15]
    (n2, act, gh, gu, gd, br, tmp) = refs[15:22]
    rest = list(refs[22:])
    d, q = here()
    nc, nd, tl, kd = plan.nc, plan.nd, plan.tl, plan.kd
    chip = q // CORES
    take = lambda n: [rest.pop(0) for _ in range(n)]
    ag = Gather(plan, n_own, n2, *take(3))
    ag_b = Gather(plan, br, branch, *take(3))
    rs = Flow(plan, *take(8))
    rs_o = Flow(plan, *take(8))
    sp_u = Spread(plan, "dp", r_u, *take(2))
    sp_d = Spread(plan, "dp", r_d, *take(2))
    (loc,) = take(1)
    greet_near(plan)
    ag.start()
    up_sum[...] = jnp.zeros_like(up_sum)
    end_chip = (chip == 0) | (chip == nc - 1)

    def process(o):
        both = pl.ds(o * CORES, CORES)
        x = n2[both].reshape(CORES * tl, plan.width)
        h = dot(x, wu[...], NN) + ub[...]
        value, slope = gelu_both(h)
        value = value.astype(BF16)
        c = cot[both].reshape(CORES * tl, plan.width)
        g = (dot(c, wd[...], NN) * slope).astype(BF16)
        act[both] = value.reshape(CORES, tl, plan.fq)
        gh[both] = g.reshape(CORES, tl, plan.fq)
        up_sum[...] += jnp.sum(g.astype(F32), axis=0, keepdims=True)
        rs.put(o, dot(g, wu[...], NT))

    def step(t, carry):
        o = nearest(plan, t)

        @pl.when(t > 0)
        def _():
            ag.arrive(o)

        @pl.when(t == 0)
        def _():
            ag.wait_own()

        ag.wait_partner(o)
        process(o)

        @pl.when(end_chip & (t >= 2))
        def _():
            rs.forward(nearest(plan, t - 1))

        return carry

    lax.fori_loop(0, nc, step, 0)
    last = nearest(plan, nc - 1)

    @pl.when(end_chip)
    def _():
        rs.forward(last)

    def weight_grad(left, right, buf, sp, sem):
        for at in range(0, plan.width, LANES):
            n = min(LANES, plan.width - at)
            a = left[:, :, at : at + n].reshape(plan.length, n)
            b = right[...].reshape(plan.length, plan.fq)
            buf[at : at + n] = dot(a, b, TN).astype(BF16)
        rows_of = lambda i: buf.at[pl.ds(pl.multiple_of(i * kd, 8), kd)]
        sp.start(rows_of)
        local(rows_of(d), sp.buf.at[d], sem).start()

    weight_grad(n2, gh, gu, sp_u, loc.at[0])
    done = lambda o: end_chip
    rs.passes(0, True, done)
    weight_grad(cot, act, gd, sp_d, loc.at[1])
    rs.passes(1, True, done)
    rs.finish(tmp)

    back, g_gain, g_shift = norm_back(resid[...], rows[0:1], tmp[...])
    total = back + c_own[...].astype(F32)
    gres[...] = total
    low = total.astype(BF16)
    br[...] = low
    ag_b.start()
    vec[0:1] = g_gain
    vec[1:2] = g_shift
    vec[2:3] = jnp.sum(low.astype(F32), axis=0, keepdims=True)

    def down(t, carry):
        o = nearest(plan, nc - 1 - t)
        a = act[pl.ds(o * CORES, CORES)].reshape(CORES * tl, plan.fq)
        rs_o.put(o, dot(a, wd[...], NT))
        return carry

    lax.fori_loop(0, nc, down, 0)
    ag_b.step(1)
    rs_o.passes(0, False)
    for s in range(2, nc):
        ag_b.step(s)
    rs_o.passes(1, False)
    rs_o.finish(tmp)
    out[...] = (resid[...] + tmp[...] + rows[1:2]).astype(BF16)
    ag_b.finish()
    ag.sent()
    rs.sent()
    rs_o.sent()
    for i, sp in enumerate((sp_u, sp_d)):
        sp.wait()
        sp.wait_sent()
        wait_for(sp.buf.at[d], loc.at[i])


def mlp_call(plan, n_own, resid, c_own, cot, wu, wd, rows, ub, ident):
    shape = jax.ShapeDtypeStruct
    nd, nq, tl, width, fq, kd = plan.nd, plan.nq, plan.tl, plan.width, plan.fq, plan.kd
    return pl.pallas_call(
        functools.partial(mlp_kernel, plan),
        out_shape=(
            shape((tl, width), BF16),
            shape((tl, width), F32),
            shape((nq, tl, width), BF16),
            shape((nd, kd, fq), BF16),
            shape((nd, kd, fq), BF16),
            shape((3, width), F32),
            shape((1, fq), F32),
        ),
        in_specs=[VMEM] * 8,
        out_specs=[VMEM, VMEM, ANY, ANY, ANY, VMEM, VMEM],
        scratch_shapes=[
            pltpu.VMEM((nq, tl, width), BF16),
            pltpu.VMEM((nq, tl, fq), BF16),
            pltpu.VMEM((nq, tl, fq), BF16),
            pltpu.VMEM((width, fq), BF16),
            pltpu.VMEM((width, fq), BF16),
            pltpu.VMEM((tl, width), BF16),
            pltpu.VMEM((tl, width), F32),
            *Gather.sems(plan),
            *Gather.sems(plan),
            *Flow.scratch(plan),
            *Flow.scratch(plan),
            dma(nd),
            dma(nd),
            dma(nd),
            dma(nd),
            dma(2),
        ],
        compiler_params=pltpu.CompilerParams(
            collective_id=ident, has_side_effects=True, vmem_limit_bytes=VMEM_LIMIT
        ),
        name="mlp",
    )(n_own, resid, c_own, cot, wu, wd, rows, ub)


def start_kernel(plan, *refs):
    (x_own, c_own, vec_own, seg_own, wq_own, wo_own, wu_own, wd_own) = refs[:8]
    (gx, gc, gv, gs, wq, wo, wu, wd) = refs[8:16]
    (zq, zo, *sem) = refs[16:]
    d, q = here()
    nd, nq, r = plan.nd, plan.nq, plan.ratio
    it = iter(sem)
    ag_x = Gather(plan, x_own, gx, next(it), next(it), next(it))
    ag_c = Gather(plan, c_own, gc, next(it), next(it), next(it))
    loc = next(it)
    sp_v = Spread(plan, "seq", gv, next(it), next(it))
    sp_s = Spread(plan, "seq", gs, next(it), next(it))
    q_send, q_recv = next(it), next(it)
    sp_q = Spread(plan, "dp", wq, next(it), next(it))
    o_send, o_recv = next(it), next(it)
    sp_o = Spread(plan, "dp", wo, next(it), next(it))
    d_send, d_recv = next(it), next(it)
    sp_d = Spread(plan, "dp", wd, next(it), next(it))
    sp_u = Spread(plan, "dp", wu, next(it), next(it))

    zq[...] = jnp.zeros_like(zq)
    zo[...] = jnp.zeros_like(zo)
    fills = [
        local(zq, wq.at[d, pl.ds((t * plan.slots + plan.slots - 1) * nq, nq)], loc.at[t])
        for t in range(3)
    ]
    fills += [
        local(zo, wo.at[d, s, pl.ds((plan.slots - 1) * nd, nd)], loc.at[3 + s]) for s in range(r)
    ]
    for fill in fills:
        fill.start()
    for fill in fills:
        fill.wait()
    greet_all(plan)

    ag_x.start()
    local(vec_own, gv.at[q], loc.at[0]).start()
    local(seg_own, gs.at[q], loc.at[1]).start()
    sp_v.start(lambda to: vec_own)
    sp_s.start(lambda to: seg_own)

    per_third = HEADS * nq
    per_dev = 3 * HEADS

    def qkv_group(j, carry):
        g = q * per_dev + j
        third = g // per_third
        rest = g - third * per_third
        head = rest // nq
        piece = rest - head * nq
        to = plan.owner(head)
        row = (third * plan.slots + head - plan.first(to)) * nq + piece
        move(wq_own.at[j], wq.at[d, row], q_send.at[j], q_recv, d, to, to == q)
        return carry

    lax.fori_loop(0, per_dev, qkv_group, 0)

    sp_u.start(lambda to: wu_own)
    local(wu_own, wu.at[d], loc.at[2]).start()

    for s in range(r):
        to_d, to_q = q // r, d * r + s
        mine = (to_d == d) & (to_q == q)
        move(
            wd_own.at[s],
            wd.at[to_d, lax.rem(q, r)],
            d_send.at[s],
            d_recv.at[lax.rem(q, r)],
            to_d,
            to_q,
            mine,
        )

    def out_group(j, carry):
        g = d * HEADS + j
        head = g // nd
        piece = g - head * nd
        to = plan.owner(head)
        row = (head - plan.first(to)) * nd + piece
        to_d = q // r
        mine = (to_d == d) & (to == q)
        move(wo_own.at[j], wo.at[to_d, lax.rem(q, r), row], o_send.at[j], o_recv, to_d, to, mine)
        return carry

    lax.fori_loop(0, HEADS, out_group, 0)
    ag_c.start()

    many = plan.count(q) == plan.slots
    few = jnp.logical_not(many)
    for cond, n in ((many, plan.slots), (few, plan.slots - 1)):

        @pl.when(cond)
        def _():
            wait_for(wq.at[0, pl.ds(0, 3 * n * nq)], q_recv)

    sp_q.start(lambda to: wq.at[d])
    ag_x.step(1)
    for cond, n in ((many, plan.slots), (few, plan.slots - 1)):

        @pl.when(cond)
        def _():
            wait_for(wo.at[0, :, pl.ds(0, n * nd)], o_recv)

    sp_o.start(lambda to: wo.at[d])
    for s in range(r):
        wait_for(wd.at[d, s], d_recv.at[s])
    sp_d.start(lambda to: wd.at[d])
    for s in range(2, plan.nc):
        ag_x.step(s)
    for s in range(1, plan.nc):
        ag_c.step(s)

    ag_x.finish()
    ag_c.finish()
    for sp in (sp_v, sp_s, sp_q, sp_o, sp_d, sp_u):
        sp.wait()
        sp.wait_sent()
    wait_for(vec_own, loc.at[0])
    wait_for(seg_own, loc.at[1])
    wait_for(wu_own, loc.at[2])

    def sent_q(j, carry):
        g = q * per_dev + j
        third = g // per_third
        head = (g - third * per_third) // nq

        @pl.when(plan.owner(head) != q)
        def _():
            wait_for(wq_own.at[0], q_send.at[j])

        return carry

    lax.fori_loop(0, per_dev, sent_q, 0)

    def sent_o(j, carry):
        to = plan.owner((d * HEADS + j) // nd)

        @pl.when(jnp.logical_not((q // r == d) & (to == q)))
        def _():
            wait_for(wo_own.at[0], o_send.at[j])

        return carry

    lax.fori_loop(0, HEADS, sent_o, 0)
    for s in range(r):

        @pl.when(jnp.logical_not((q // r == d) & (d * r + s == q)))
        def _():
            wait_for(wd_own.at[s], d_send.at[s])


def start_call(plan, x, c, vec, seg, wq, wo, wu, wd):
    nd, nq, r = plan.nd, plan.nq, plan.ratio
    shape = jax.ShapeDtypeStruct
    outs = (
        shape((nq, *x.shape), x.dtype),
        shape((nq, *c.shape), c.dtype),
        shape((nq, *vec.shape), vec.dtype),
        shape((nq, *seg.shape), seg.dtype),
        shape((nd, plan.groups_q, plan.gq, plan.kd), BF16),
        shape((nd, r, plan.groups_o, plan.go, plan.cq), BF16),
        shape((nd, *wu.shape), BF16),
        shape((nd, *wd.shape), BF16),
    )
    return pl.pallas_call(
        functools.partial(start_kernel, plan),
        out_shape=outs,
        in_specs=[VMEM] * 8,
        out_specs=[ANY] * 8,
        scratch_shapes=[
            pltpu.VMEM((nq, plan.gq, plan.kd), BF16),
            pltpu.VMEM((nd, plan.go, plan.cq), BF16),
            *Gather.sems(plan),
            *Gather.sems(plan),
            dma(3 + r),
            dma(nq),
            dma(nq),
            dma(nq),
            dma(nq),
            dma(3 * HEADS),
            pltpu.SemaphoreType.DMA,
            dma(nd),
            dma(nd),
            dma(HEADS),
            pltpu.SemaphoreType.DMA,
            dma(nd),
            dma(nd),
            dma(r),
            dma(r),
            dma(nd),
            dma(nd),
            dma(nd),
            dma(nd),
        ],
        compiler_params=pltpu.CompilerParams(
            collective_id=0, has_side_effects=True, vmem_limit_bytes=VMEM_LIMIT
        ),
        name="start",
    )(x, c, vec, seg, wq, wo, wu, wd)


def gather_kernel(plan, own, buf, *sem):
    greet_chain(plan)
    ag = Gather(plan, own, buf, *sem)
    ag.start()
    for s in range(1, plan.nc):
        ag.step(s)
    ag.finish()


def gather_call(plan, own, ident):
    return pl.pallas_call(
        functools.partial(gather_kernel, plan),
        out_shape=jax.ShapeDtypeStruct((plan.nq, *own.shape), own.dtype),
        in_specs=[VMEM],
        out_specs=ANY,
        scratch_shapes=Gather.sems(plan),
        compiler_params=pltpu.CompilerParams(
            collective_id=ident, has_side_effects=True, vmem_limit_bytes=VMEM_LIMIT
        ),
        name="gather",
    )(own)


def scatter_kernel(plan, n, *refs):
    parts, outs, scratch = refs[:n], refs[n : 2 * n], refs[2 * n :]
    greet_chain(plan)
    each = len(scratch) // n
    rs = [
        Scatter(plan, parts[i], *scratch[i * each : i * each + 3], scratch[i * each + 3 : (i + 1) * each])
        for i in range(n)
    ]
    for one in rs:
        one.start()
    for one in rs:
        one.flows()
    for one, out in zip(rs, outs):
        one.finish(out)


def scatter_call(plan, parts, ident):
    n = len(parts)
    return pl.pallas_call(
        functools.partial(scatter_kernel, plan, n),
        out_shape=[jax.ShapeDtypeStruct((plan.tl, plan.width), F32)] * n,
        in_specs=[VMEM] * n,
        out_specs=[VMEM] * n,
        scratch_shapes=Scatter.scratch(plan) * n,
        compiler_params=pltpu.CompilerParams(
            collective_id=ident, has_side_effects=True, vmem_limit_bytes=VMEM_LIMIT
        ),
        name="scatter",
    )(*parts)


def end_kernel(plan, *refs):
    (p_n1, s_d, g_q, g_o) = refs[:4]
    (out_n1, o_d, o_q, o_o) = refs[4:8]
    (r_q, r_o, s_q, s_o) = refs[8:12]
    swap, flow, run, *rest = refs[12:]
    rs_sems, sem = rest[:4], rest[4:]
    d, q = here()
    nd, nq, r = plan.nd, plan.nq, plan.ratio
    it = iter(sem)
    sp = [Spread(plan, "dp", buf, next(it), next(it)) for buf in (r_q, r_o)]
    loc = next(it)
    d_send, d_recv, q_send, q_recv, o_send, o_recv = (next(it) for _ in range(6))
    rs = Scatter(plan, p_n1, swap, flow, run, rs_sems)

    greet_all(plan)
    rs.start()
    parts = (g_q, g_o)
    for i in (0, 1):
        sp[i].start(lambda to, i=i: parts[i].at[to])
        local(parts[i].at[d], sp[i].buf.at[d], loc.at[i]).start()
    for s in range(r):
        to_d, to_q = q // r, d * r + s
        mine = (to_d == d) & (to_q == q)
        move(
            s_d.at[s], o_d.at[lax.rem(q, r)], d_send.at[s], d_recv.at[lax.rem(q, r)], to_d, to_q, mine
        )

    rs.flows()
    per_third = HEADS * nq
    per_dev = 3 * HEADS
    sp[0].wait()
    wait_for(r_q.at[d], loc.at[0])
    first, count = plan.first(q), plan.count(q)

    def qkv_group(k, carry):
        total = r_q[0, k].astype(F32)
        for i in range(1, nd):
            total += r_q[i, k].astype(F32)
        s_q[k] = total.astype(BF16)
        return carry

    lax.fori_loop(0, plan.groups_q, qkv_group, 0)

    def qkv_place(k):
        third = k // (plan.slots * nq)
        rest = k - third * (plan.slots * nq)
        slot = rest // nq
        g = third * per_third + first * nq + rest
        to = g // per_dev
        return slot, to, g - to * per_dev

    def qkv_send(k, carry):
        slot, to, j = qkv_place(k)

        @pl.when(slot < count)
        def _():
            move(s_q.at[k], o_q.at[j], q_send.at[k], q_recv, d, to, to == q)

        return carry

    lax.fori_loop(0, plan.groups_q, qkv_send, 0)

    sp[1].wait()
    wait_for(r_o.at[d], loc.at[1])

    def out_place(k):
        slot = k // nd
        g = first * nd + k
        to_d = g // HEADS
        return slot, to_d, g - to_d * HEADS

    for s in range(r):

        def out_group(k, carry):
            total = r_o[0, s, k].astype(F32)
            for i in range(1, nd):
                total += r_o[i, s, k].astype(F32)
            s_o[s, k] = total.astype(BF16)
            return carry

        lax.fori_loop(0, plan.groups_o, out_group, 0)

    for s in range(r):

        def out_send(k, carry):
            slot, to_d, j = out_place(k)
            to_q = d * r + s
            mine = (to_d == d) & (to_q == q)

            @pl.when(slot < count)
            def _():
                move(s_o.at[s, k], o_o.at[j], o_send.at[s, k], o_recv, to_d, to_q, mine)

            return carry

        lax.fori_loop(0, plan.groups_o, out_send, 0)

    rs.finish(out_n1)
    for s in range(r):
        wait_for(o_d.at[s], d_recv.at[s])
    wait_for(o_q, q_recv)
    wait_for(o_o, o_recv)
    for one in sp:
        one.wait_sent()

    for s in range(r):

        @pl.when(jnp.logical_not((q // r == d) & (d * r + s == q)))
        def _():
            wait_for(s_d.at[s], d_send.at[s])

    def sent_q(k, carry):
        slot, to, j = qkv_place(k)

        @pl.when((slot < count) & (to != q))
        def _():
            wait_for(s_q.at[0], q_send.at[k])

        return carry

    lax.fori_loop(0, plan.groups_q, sent_q, 0)
    for s in range(r):

        def sent_o(k, carry):
            slot, to_d, j = out_place(k)
            mine = (to_d == d) & (d * r + s == q)

            @pl.when((slot < count) & jnp.logical_not(mine))
            def _():
                wait_for(s_o.at[0, 0], o_send.at[s, k])

            return carry

        lax.fori_loop(0, plan.groups_o, sent_o, 0)


def end_call(plan, p_n1, g_d, g_q, g_o, ident):
    nd, nq, r = plan.nd, plan.nq, plan.ratio
    shape = jax.ShapeDtypeStruct
    return pl.pallas_call(
        functools.partial(end_kernel, plan),
        out_shape=(
            shape((plan.tl, plan.width), F32),
            shape(g_d.shape, BF16),
            shape((3 * HEADS, plan.gq, plan.kd), BF16),
            shape((HEADS, plan.go, plan.cq), BF16),
        ),
        in_specs=[VMEM, ANY, ANY, ANY],
        out_specs=[VMEM, ANY, ANY, ANY],
        scratch_shapes=[
            pltpu.VMEM(g_q.shape, BF16),
            pltpu.VMEM(g_o.shape, BF16),
            pltpu.VMEM(g_q.shape[1:], BF16),
            pltpu.VMEM(g_o.shape[1:], BF16),
            *Scatter.scratch(plan),
            *[dma(nd)] * 4,
            dma(2),
            dma(r),
            dma(r),
            dma(plan.groups_q),
            pltpu.SemaphoreType.DMA,
            dma(r, plan.groups_o),
            pltpu.SemaphoreType.DMA,
        ],
        compiler_params=pltpu.CompilerParams(
            collective_id=ident, has_side_effects=True, vmem_limit_bytes=VMEM_LIMIT
        ),
        name="end",
    )(p_n1, g_d, g_q, g_o)


def vector_kernel(plan, v_own, u_own, v_out, u_out, r_seq, r_dp, r_u, mid, *sem):
    d, q = here()
    greet_all(plan)
    it = iter(sem)
    sp_s = Spread(plan, "seq", r_seq, next(it), next(it))
    sp_d = Spread(plan, "dp", r_dp, next(it), next(it))
    sp_u = Spread(plan, "dp", r_u, next(it), next(it))
    sp_u.start(lambda to: u_own)
    sp_s.start(lambda to: v_own.at[to])
    sp_s.wait()
    total = v_own[q]
    for k in range(1, plan.nq):
        total += r_seq[sp_s.other(k)]
    mid[...] = total
    sp_d.start(lambda to: mid)
    sp_u.wait()
    sum_u = u_own[...]
    for k in range(1, plan.nd):
        sum_u += r_u[sp_u.other(k)]
    u_out[...] = sum_u
    sp_d.wait()
    for k in range(1, plan.nd):
        total += r_dp[sp_d.other(k)]
    v_out[...] = total
    for one in (sp_s, sp_d, sp_u):
        one.wait_sent()


def vector_call(plan, v, u, ident):
    nd, nq = plan.nd, plan.nq
    shape = jax.ShapeDtypeStruct
    return pl.pallas_call(
        functools.partial(vector_kernel, plan),
        out_shape=(shape(v.shape[1:], F32), shape(u.shape, F32)),
        in_specs=[VMEM] * 2,
        out_specs=[VMEM] * 2,
        scratch_shapes=[
            pltpu.VMEM(v.shape, F32),
            pltpu.VMEM((nd, *v.shape[1:]), F32),
            pltpu.VMEM((nd, *u.shape), F32),
            pltpu.VMEM(v.shape[1:], F32),
            dma(nq),
            dma(nq),
            dma(nd),
            dma(nd),
            dma(nd),
            dma(nd),
        ],
        compiler_params=pltpu.CompilerParams(
            collective_id=ident, has_side_effects=True, vmem_limit_bytes=VMEM_LIMIT
        ),
        name="vectors",
    )(v, u)


ROWS = 256


def visible(segc, segr, at, start, rows, keys):
    seen = segc[at : at + rows] == segr[:, start : start + keys]
    qpos = at + lax.broadcasted_iota(jnp.int32, (rows, keys), 0)
    kpos = start + lax.broadcasted_iota(jnp.int32, (rows, keys), 1)
    return seen & (kpos <= qpos)


def only(half, values):
    lane = lax.broadcasted_iota(jnp.int32, values.shape, 1)
    keep = (lane < HEAD_DIM) if half == 0 else (lane >= HEAD_DIM)
    return jnp.where(keep, values, jnp.zeros_like(values))


def either(first, second):
    lane = lax.broadcasted_iota(jnp.int32, first.shape, 1)
    return jnp.where(lane < HEAD_DIM, first, second)


def attend_kernel(plan, q_ref, k_ref, v_ref, segc, segr, o_ref, lse_ref):
    length, most = plan.length, plan.length // 2
    for at in range(0, length, ROWS):
        start = max(0, at - most)
        keys = at + ROWS - start
        mask = visible(segc, segr, at, start, ROWS, keys)
        query = q_ref[at : at + ROWS]
        key, value = k_ref[start : start + keys], v_ref[start : start + keys]
        outs, logs = [], []
        for half in range(2):
            scores = dot(only(half, query), key, NT) * (HEAD_DIM**-0.5)
            scores = jnp.where(mask, scores, -1e30)
            top = jnp.max(scores, axis=-1, keepdims=True)
            weights = jnp.exp(scores - top)
            total = jnp.sum(weights, axis=-1, keepdims=True)
            probs = (weights * (1.0 / total)).astype(BF16)
            outs.append(dot(probs, value, NN))
            logs.append(jnp.broadcast_to(top + jnp.log(total), (ROWS, 2 * HEAD_DIM)))
        o_ref[at : at + ROWS] = either(*outs).astype(BF16)
        lse_ref[at : at + ROWS] = either(*logs)


def attend_call(plan, mixed, segc, segr):
    pairs = plan.slots // 2
    block = lambda third: pl.BlockSpec((plan.length, 128), lambda i: (0, third * pairs + i))
    whole = lambda a: pl.BlockSpec(a.shape, lambda i: (0, 0))
    return pl.pallas_call(
        functools.partial(attend_kernel, plan),
        grid=(pairs,),
        out_shape=(
            jax.ShapeDtypeStruct((plan.length, plan.hw), BF16),
            jax.ShapeDtypeStruct((plan.length, plan.hw), F32),
        ),
        in_specs=[block(0), block(1), block(2), whole(segc), whole(segr)],
        out_specs=[block(0), block(0)],
        compiler_params=pltpu.CompilerParams(vmem_limit_bytes=VMEM_LIMIT),
        name="attend",
    )(mixed, mixed, mixed, segc, segr)


def attend_back_kernel(plan, q_ref, k_ref, v_ref, g_ref, lse_ref, segc, segr, dq, dk, dv, ak, av):
    length, most = plan.length, plan.length // 2
    scaling = HEAD_DIM**-0.5
    ak[...] = jnp.zeros_like(ak)
    av[...] = jnp.zeros_like(av)
    for at in range(0, length, ROWS):
        start = max(0, at - most)
        keys = at + ROWS - start
        mask = visible(segc, segr, at, start, ROWS, keys)
        query, grad = q_ref[at : at + ROWS], g_ref[at : at + ROWS]
        key, value = k_ref[start : start + keys], v_ref[start : start + keys]
        outs = []
        for half in range(2):
            query_h, grad_h = only(half, query), only(half, grad)
            scores = dot(query_h, key, NT) * scaling
            scores = jnp.where(mask, scores, -1e30)
            log = lse_ref[at : at + ROWS, half * HEAD_DIM : half * HEAD_DIM + 1]
            probs = jnp.exp(scores - log)
            grad_probs = dot(grad_h, value, NT)
            delta = jnp.sum(probs * grad_probs, axis=-1, keepdims=True)
            grad_scores = (probs * (grad_probs - delta)).astype(BF16)
            outs.append(dot(grad_scores, key, NN))
            ak[start : start + keys] += dot(grad_scores, query_h, TN)
            av[start : start + keys] += dot(probs.astype(BF16), grad_h, TN)
        dq[at : at + ROWS] = (either(*outs) * scaling).astype(BF16)
    dk[...] = (ak[...] * scaling).astype(BF16)
    dv[...] = av[...].astype(BF16)


def attend_back_call(plan, mixed, grad, lse, segc, segr):
    pairs = plan.slots // 2
    block = lambda third: pl.BlockSpec((plan.length, 128), lambda i: (0, third * pairs + i))
    whole = lambda a: pl.BlockSpec(a.shape, lambda i: (0, 0))
    return pl.pallas_call(
        functools.partial(attend_back_kernel, plan),
        grid=(pairs,),
        out_shape=[jax.ShapeDtypeStruct((plan.length, plan.hw), BF16)] * 3,
        in_specs=[block(0), block(1), block(2), block(0), block(0), whole(segc), whole(segr)],
        out_specs=[block(0)] * 3,
        scratch_shapes=[pltpu.VMEM((plan.length, 128), F32)] * 2,
        compiler_params=pltpu.CompilerParams(vmem_limit_bytes=VMEM_LIMIT),
        name="attend_back",
    )(mixed, mixed, mixed, grad, lse, segc, segr)


def shards(
    nd,
    nq,
    inputs,
    segment_ids,
    cotangent,
    attn_gain,
    attn_shift,
    qkv_weight,
    query_bias,
    value_bias,
    out_weight,
    out_bias,
    mlp_gain,
    mlp_shift,
    up_weight,
    up_bias,
    down_weight,
    down_bias,
):
    width = inputs.shape[2]
    plan = Plan(nd, nq, inputs.shape[1], width, up_weight.shape[1] * nq)
    r, slots, length = plan.ratio, plan.slots, plan.length
    q = lax.axis_index("seq")
    first, count = plan.first(q), plan.count(q)

    vec = jnp.stack(
        [attn_gain, attn_shift, query_bias, value_bias, out_bias, mlp_gain, mlp_shift, down_bias]
    )
    got = start_call(
        plan,
        inputs[0],
        cotangent[0],
        vec,
        segment_ids,
        qkv_weight.T.reshape(3 * HEADS, plan.gq, plan.kd),
        out_weight.reshape(HEADS, plan.go, plan.cq),
        up_weight,
        down_weight.T.reshape(plan.cq, r, plan.fq).transpose(1, 0, 2),
    )
    gx, gc, gv, gs, wq, wo, wu, wd = got
    xs = gx.reshape(length, width).astype(F32)
    cot = gc.reshape(length, width)
    v = gv.transpose(1, 0, 2).reshape(8, width).astype(F32)
    gain_one, shift_one, bias_query, bias_value, bias_out, gain_two, shift_two, bias_down = v
    segr = gs.reshape(1, length)
    segc = gs.reshape(length, 1)
    wq = wq.reshape(nd, 3 * plan.hw, plan.kd).transpose(1, 0, 2).reshape(3 * plan.hw, width)
    wo = wo.reshape(nd, r, plan.hw, plan.cq).transpose(2, 0, 1, 3).reshape(plan.hw, width)
    wu = wu.reshape(width, plan.fq)
    wd = wd.reshape(width, plan.fq)

    normed = layer_norm(xs, gain_one, shift_one).astype(BF16)
    mine = lambda b: lax.dynamic_slice(jnp.pad(b, (0, plan.hw)), (first * HEAD_DIM,), (plan.hw,))
    biases = jnp.concatenate([mine(bias_query), jnp.zeros((plan.hw,), F32), mine(bias_value)])
    mixed = (dot(normed, wq, NT) + biases).astype(BF16)
    attended, lse = attend_call(plan, mixed, segc, segr)
    part = dot(attended, wo, NN).astype(BF16).reshape(nq, plan.tl, width)
    (branch,) = scatter_call(plan, [part], 1)
    stream = inputs[0].astype(F32)
    residual = stream + branch + bias_out
    second = layer_norm(residual, gain_two, shift_two).astype(BF16)
    rows = jnp.stack([gain_two, bias_down])
    output, grad_resid, branch_all, r_u, r_d, sums, up_sum = mlp_call(
        plan, second, residual, cotangent[0], gc, wu, wd, rows, up_bias.astype(F32)[None], 2
    )
    top = cotangent[0].astype(F32)
    branch_all = branch_all.reshape(length, width)
    grad_attended = dot(branch_all, wo, NT).astype(BF16)
    dq, dk, dv = attend_back_call(plan, mixed, grad_attended, lse, segc, segr)
    grad_mixed = jnp.concatenate([dq, dk, dv], axis=1)
    part_one = dot(grad_mixed, wq, NN).astype(BF16).reshape(nq, plan.tl, width)

    g_q = dot(grad_mixed, normed, TN).astype(BF16).reshape(3 * plan.hw, nd, plan.kd)
    g_q = g_q.transpose(1, 0, 2).reshape(nd, plan.groups_q, plan.gq, plan.kd)
    g_o = dot(attended, branch_all, TN).astype(BF16).reshape(plan.hw, nd, r, plan.cq)
    g_o = g_o.transpose(1, 2, 0, 3).reshape(nd, r, plan.groups_o, plan.go, plan.cq)
    g_d = jnp.sum(r_d.astype(F32), axis=0).astype(BF16).reshape(r, plan.cq, plan.fq)
    grad_normed, o_d, o_q, o_o = end_call(plan, part_one, g_d, g_q, g_o, 5)
    grad_stream, grad_gain_one, grad_shift_one = jax.vjp(layer_norm, stream, gain_one, shift_one)[
        1
    ](grad_normed)
    grad_input = grad_stream + grad_resid

    def spread_heads(grad):
        sums = jnp.sum(grad.astype(F32), axis=0)
        sums = jnp.where(jnp.arange(plan.hw) < count * HEAD_DIM, sums, 0.0)
        full = jnp.zeros((width + plan.hw,), F32)
        return lax.dynamic_update_slice(full, sums, (first * HEAD_DIM,))[:width]

    vectors = jnp.stack(
        [
            grad_gain_one,
            grad_shift_one,
            spread_heads(dq),
            spread_heads(dv),
            sums[2],
            sums[0],
            sums[1],
            jnp.sum(top, axis=0),
        ]
    )
    vectors = vectors.reshape(8, nq, plan.cq).transpose(1, 0, 2)
    vectors, up_sum = vector_call(plan, vectors, up_sum, 6)
    grad_up = jnp.sum(r_u.astype(F32), axis=0)
    grad_down = o_d.astype(F32).transpose(0, 2, 1).reshape(r * plan.fq, plan.cq)
    grad_qkv = o_q.astype(F32).reshape(3 * HEADS * plan.gq, plan.kd).T
    grad_out = o_o.astype(F32).reshape(plan.kd, plan.cq)
    return (
        output[None],
        grad_input[None],
        vectors[0],
        vectors[1],
        grad_qkv,
        vectors[2],
        vectors[3],
        grad_out,
        vectors[4],
        vectors[5],
        vectors[6],
        grad_up,
        up_sum[0],
        grad_down,
        vectors[7],
    )


def solution(mesh):
    tokens, vector, matrix = P("dp", "seq", None), P("seq"), P("dp", "seq")
    return jax.shard_map(
        functools.partial(shards, mesh.shape["dp"], mesh.shape["seq"]),
        mesh=mesh,
        in_specs=(
            tokens,
            matrix,
            tokens,
            vector,
            vector,
            matrix,
            vector,
            vector,
            matrix,
            vector,
            vector,
            vector,
            matrix,
            vector,
            matrix,
            vector,
        ),
        out_specs=(
            tokens,
            tokens,
            vector,
            vector,
            matrix,
            vector,
            vector,
            matrix,
            vector,
            vector,
            vector,
            matrix,
            vector,
            matrix,
            vector,
        ),
        check_vma=False,
    )
```
